32 devices in a mesh: groups: 1, expert: 8 (over z, y), dp: 4 (over x, core).
Axes of the slice: x: 2, y: 2, z: 4, core: 2. Of those that a mesh axis runs over, the one named last changes fastest.
Arguments:
- queries: bfloat16 [2048, 4096], P(('groups', 'dp'), 'expert'), may hold values from -6 to 6
- keys_in: bfloat16 [2048, 4096], P(('groups', 'dp'), 'expert'), may hold values from -6 to 6
- values_in: bfloat16 [2048, 4096], P(('groups', 'dp'), 'expert'), may hold values from -6 to 6
- gate_in: bfloat16 [2048, 4096], P(('groups', 'dp'), 'expert'), may hold values from -6 to 6
- beta: float32 [2048, 32], P(('groups', 'dp'), 'expert'), may hold values from 0.1 to 1
- decay: float32 [2048, 32], P(('groups', 'dp'), 'expert'), may hold values from -1 to 0
- lengths: int32 [4, 4], P(('groups', 'dp')), may hold values from 1 to 256, 512 in all within a row
- cache: float32 [16, 32, 128, 128], P(('groups', 'dp'), 'expert'), may hold values from -6 to 6
- norm_gain: float32 [128], replicated, may hold values from 0.1 to 1.9
- out_proj: bfloat16 [4096, 2048], P('expert'), may hold values from -0.09375 to 0.09375
- residual: bfloat16 [2048, 2048], P(('groups', 'dp', 'expert')), may hold values from -6 to 6
- post_gain: float32 [2048], replicated, may hold values from 0.1 to 1.9
- expert_ids: int32 [2048, 10], P(('groups', 'dp', 'expert')), may hold values from 0 to 31, all different within a row; in each aligned block of 64 rows (0 to 63, 64 to 127, ...) at most 25 rows name the same one
- route_weights: float32 [2048, 10], P(('groups', 'dp', 'expert')), may hold values from 0.05 to 1
- gate_up: bfloat16 [32, 2048, 512], P(('expert', 'dp')), may hold values from -0.125 to 0.125
- down_proj: bfloat16 [32, 256, 2048], P(('expert', 'dp')), may hold values from -0.375 to 0.375
Outputs:
- moe_out: bfloat16 [2048, 2048], P(('groups', 'dp', 'expert'))
- attn_out: bfloat16 [2048, 2048], P(('groups', 'dp', 'expert'))
- new_states: float32 [16, 32, 128, 128], P(('groups', 'dp'), 'expert')
The draws below stay inside these ranges and needn't reach their ends.
Inputs may be any that keep to these rules, and one draw needn't show every extreme that they name: Each row of lengths fills its shard's 512 rows; the longest span of each row is exactly 256. `expert_ids`: each row names 10 different experts. Within the 64 rows of one device no expert is named more than 25 times, a bound that some block reaches; every expert is named somewhere.
All inputs are finite; a program needn't handle non-finite values.
Results may differ from the reference program's by a relative error of at most 0.025.
Values may be sent and summed in bfloat16 or wider, within the bound.
No kernel may reach another device: no remote copies, remote signals or barrier semaphores. Data moves between devices by JAX's collectives and lax.ppermute only.
A program may use at most 64 MiB of HBM per device.

```python
import math
import jax
import jax.numpy as jnp
import numpy as np
from jax import lax

D = 2048
HEAD = 128
VALUE_HEADS = 32
TOP = 10
FF = 256
SPAN_MAX = 256
TOK_DP = 512
REQ_DP = 4
TOK_DEV = 64
TOKEN_ROWS_ALL = 2048
REQS = 16
SHARDS = 4
EXPERTS = 32
CAP = 25
N_EXPERT = 8
N_DP = 4


def draw_decay(key, part):
    base = jax.random.fold_in(key, 11)
    request_flows = jax.random.split(base, 6)
    share = 0.4
    fast = jax.random.uniform(request_flows[0], (VALUE_HEADS,)) < share
    fast_rate = jnp.exp(jax.random.uniform(request_flows[1], (VALUE_HEADS,), minval=math.log(1.0 / 50.0), maxval=math.log(1.0 / 30.0)))
    slow_rate = jnp.exp(jax.random.uniform(request_flows[2], (VALUE_HEADS,), minval=math.log(0.001), maxval=math.log(0.004)))
    arrival_rates = jnp.where(fast, fast_rate, slow_rate)
    random_wobble = jnp.exp(jax.random.uniform(request_flows[3], (TOKEN_ROWS_ALL, VALUE_HEADS), minval=math.log(0.5), maxval=math.log(2.0)))
    surge_token_rows = jax.random.uniform(request_flows[4], (TOKEN_ROWS_ALL, 1)) < 1.0 / 64.0
    surge_length = jax.random.uniform(request_flows[5], (TOKEN_ROWS_ALL, VALUE_HEADS), minval=0.22, maxval=0.7)
    grand_count = arrival_rates[None, :] * random_wobble + jnp.where(surge_token_rows, surge_length, 0.0)
    return (-grand_count).astype(jnp.float32)


def level_of(key, dims, cuts, smallest, high):
    def one(position, blocks):
        steps = jax.random.uniform(jax.random.fold_in(jax.random.fold_in(key, 6), position), (blocks,), jnp.float32, smallest / len(cuts), high / len(cuts))
        return jnp.repeat(jnp.exp(steps), dims[position] // blocks).reshape((-1,) + (1,) * (len(dims) - position - 1))

    level = one(*cuts[0])
    for cut in cuts[1:]:
        level = level * one(*cut)
    return level


def length_profile(count, total, most, lean):
    portions = [(1 << 20) // math.isqrt(grade ** lean) + 1 for grade in range(2, count + 1)]
    surplus, given = total - most - (count - 1), [1] * (count - 1)
    while surplus > 0:
        movable = [i for i in range(count - 1) if given[i] < most]
        mass, left = sum([portions[i] for i in movable]), surplus
        for i in movable:
            more = min(most - given[i], max(1, left * portions[i] // mass), surplus)
            given[i] = given[i] + more
            surplus = surplus - more
    return np.array([most] + given)


def ragged(key, count, total, reach, slope):
    if count == 2:
        one = jax.random.randint(key, (), max(1, total - reach), min(reach, total - 1) + 1)
        return jnp.stack([one, total - one])
    sizes = jnp.asarray(length_profile(count, total, reach, slope), jnp.int32)
    twos = (count - 1) // 2
    giver, receiver = sizes[1:1 + 2 * twos:2], sizes[2:2 + 2 * twos:2]
    room = jnp.minimum(giver - 1, reach - receiver)
    shifted = jax.random.randint(jax.random.fold_in(key, 1), (twos,), 0, 1 << 20) % (room + 1)
    sizes = sizes.at[1:1 + 2 * twos:2].set(giver - shifted).at[2:2 + 2 * twos:2].set(receiver + shifted)
    return sizes[jax.random.permutation(jax.random.fold_in(key, 2), count)]


def shared_out(stream_key, own, number, rows, count, top, bound, lean):
    order = jax.random.permutation(stream_key, count)
    heavy_load, ordinary = shares(count, rows * top, bound, lean, True), shares(count, rows * top, bound, lean, False)
    places = jnp.arange(count)

    def named(sizes, offset_by):
        used = int((sizes > 0).sum())
        fixed = max(1, used // 4)
        passed = fixed + (places - fixed + offset_by * (used - fixed)) % max(1, count - fixed)
        return jnp.zeros((count,), jnp.int32).at[order[jnp.where(places < fixed, places, passed)]].set(jnp.asarray(sizes, jnp.int32))

    sizes = jnp.where(number % 4 == 0, named(heavy_load, number // 4), named(ordinary, number - number // 4 - 1))
    mixed = jax.random.permutation(jax.random.fold_in(own, 3), count)
    giver, taker = mixed[0:count // 2 * 2:2], mixed[1:count // 2 * 2:2]
    slack = jnp.minimum(sizes[giver] - 1, bound - sizes[taker]) // 2
    slack = jnp.where((giver == order[0]) | (taker == order[0]) | (sizes[taker] == 0), 0, jnp.maximum(slack, 0))
    passed = jax.random.randint(jax.random.fold_in(own, 4), (count // 2,), 0, 1 << 20) % (slack + 1)
    sizes = sizes.at[giver].add(-passed).at[taker].add(passed)
    labels = jnp.searchsorted(jnp.cumsum(sizes), jnp.arange(rows * top), side="right").astype(jnp.int32)
    listing = labels.reshape(top, rows).T
    listing = listing[jax.random.permutation(jax.random.fold_in(own, 1), rows)]
    offset_by = jax.random.randint(jax.random.fold_in(own, 2), (rows, 1), 0, top)
    return jnp.take_along_axis(listing, (jnp.arange(top)[None, :] + offset_by) % top, axis=1)


def shares(number_of, total, bound, slope, full):
    weights = [(1 << 20) // math.isqrt(standing ** slope) + 1 for standing in range(1, number_of + 1)]
    largest = bound if full else min(bound, max(-(-total // number_of), total * weights[0] // sum(weights)))
    least = 1 if total - largest >= number_of - 1 else 0
    holding, spare = [largest] + [least] * (number_of - 1), total - largest - least * (number_of - 1)
    while spare > 0:
        candidates = [i for i in range(1, number_of) if holding[i] < largest] or [i for i in range(1, number_of) if holding[i] < bound]
        whole, left = sum([weights[i] for i in candidates]), spare
        for i in candidates:
            extra = min(bound - holding[i], max(1, left * weights[i] // whole), spare)
            holding[i] = holding[i] + extra
            spare = spare - extra
    return np.array(holding)


def normal_values(own_key, extent, spread, most, cuts=(), held_as=jnp.bfloat16):
    entries = jax.random.normal(own_key, extent, jnp.float32) * spread
    if len(cuts) > 0:
        entries = level_of(own_key, extent, cuts, -0.22, 0.18) * entries
    return jnp.clip(entries, min=-most, max=most).astype(held_as)


def setup_inputs(seed: int = 0, part: int = 0) -> dict:
    streams_of = jax.random.split(jax.random.key(seed), 17)
    part_splits = jax.random.split(jax.random.fold_in(streams_of[16], part), 17)
    queries = normal_values(part_splits[0], (TOKEN_ROWS_ALL, VALUE_HEADS * HEAD), 1.0, 6.0, ((0, 4), (1, 8)))
    keys_in = normal_values(part_splits[1], (TOKEN_ROWS_ALL, VALUE_HEADS * HEAD), 1.0, 6.0, ((0, 4), (1, 8)))
    values_in = normal_values(part_splits[2], (TOKEN_ROWS_ALL, VALUE_HEADS * HEAD), 1.0, 6.0, ((0, 4), (1, 8)))
    gate_in = normal_values(part_splits[3], (TOKEN_ROWS_ALL, VALUE_HEADS * HEAD), 1.0, 6.0, ((0, 4), (1, 8)))
    beta = jnp.clip(0.1 + 0.9 * jax.random.uniform(part_splits[4], (TOKEN_ROWS_ALL, VALUE_HEADS), jnp.float32) ** level_of(part_splits[4], (TOKEN_ROWS_ALL, VALUE_HEADS), ((0, 4), (1, 8)), -0.2, 0.2), 0.1, 1.0)
    decay = draw_decay(jax.random.fold_in(jax.random.fold_in(streams_of[16], part), 71), part)
    lengths = jax.vmap(lambda own: ragged(own, REQ_DP, TOK_DP, SPAN_MAX, 2))(jax.random.split(part_splits[6], SHARDS)).reshape((SHARDS, REQ_DP)).astype(jnp.int32)
    cache = normal_values(part_splits[7], (REQS, VALUE_HEADS, HEAD, HEAD), 1.0, 6.0, ((0, 4), (1, 8)), jnp.float32)
    norm_gain = jnp.clip(1.0 + 0.18 * jax.random.normal(streams_of[8], (HEAD,), jnp.float32), 0.1, 1.9)
    out_proj = normal_values(streams_of[9], (VALUE_HEADS * HEAD, D), (VALUE_HEADS * HEAD) ** -0.5, 0.09375, ((0, 8),))
    residual = normal_values(part_splits[10], (TOKEN_ROWS_ALL, D), 1.0, 6.0, ((0, 32),))
    post_gain = jnp.clip(1.0 + 0.18 * jax.random.normal(streams_of[11], (D,), jnp.float32), 0.1, 1.9)
    expert_ids_keys = jax.random.split(jax.random.fold_in(part_splits[12], 1), TOKEN_ROWS_ALL // TOK_DEV)
    expert_ids_turns = jax.random.permutation(jax.random.fold_in(part_splits[12], 3), TOKEN_ROWS_ALL // TOK_DEV)
    expert_ids = jax.vmap(lambda own, number: shared_out(jax.random.fold_in(part_splits[12], 2), own, number, TOK_DEV, EXPERTS, TOP, CAP, 2))(expert_ids_keys, expert_ids_turns).reshape((TOKEN_ROWS_ALL, TOP))
    route_weights = jnp.clip(jnp.exp(math.log(1.0) - 2.9957323 * jax.random.uniform(part_splits[13], (TOKEN_ROWS_ALL, TOP), jnp.float32) ** level_of(part_splits[13], (TOKEN_ROWS_ALL, TOP), ((0, 32),), -0.2, 0.2)), 0.05, 1.0)
    gate_up = normal_values(streams_of[14], (EXPERTS, D, 2 * FF), D ** -0.5, 0.125, ((0, 32),))
    down_proj = normal_values(streams_of[15], (EXPERTS, FF, D), FF ** -0.5, 0.375, ((0, 32),))
    return dict(queries=queries, keys_in=keys_in, values_in=values_in, gate_in=gate_in, beta=beta, decay=decay, lengths=lengths, cache=cache, norm_gain=norm_gain, out_proj=out_proj, residual=residual, post_gain=post_gain, expert_ids=expert_ids, route_weights=route_weights, gate_up=gate_up, down_proj=down_proj)


HIGH = lax.Precision.HIGHEST
epsilon = 1e-06

def unit_rows(values):
    return values * lax.rsqrt(lax.optimization_barrier(jnp.sum(values * values, axis=-1, keepdims=True)) + epsilon)

def reference(queries, keys_in, values_in, gate_in, beta, decay, lengths, cache, norm_gain, out_proj, residual, post_gain, expert_ids, route_weights, gate_up, down_proj):
    shards = lengths.shape[0]
    layout = (shards, TOK_DP, VALUE_HEADS, HEAD)
    query_n = unit_rows(queries.astype(jnp.float32).reshape(layout)) * HEAD ** (-0.5)
    key_n = unit_rows(keys_in.astype(jnp.float32).reshape(layout))
    value_f = values_in.astype(jnp.float32).reshape(layout)
    beta_s = beta.reshape(shards, TOK_DP, VALUE_HEADS)
    decay_s = decay.reshape(shards, TOK_DP, VALUE_HEADS)
    ends = jnp.cumsum(lengths, axis=1).astype(jnp.int32)
    starts = (ends - lengths).astype(jnp.int32)
    places = jnp.arange(TOK_DP, dtype=jnp.int32)
    request = lax.optimization_barrier(jnp.sum((places[None, :, None] >= ends[:, None, :]).astype(jnp.int32), axis=2)).astype(jnp.int32)
    first_row = jnp.any(places[None, :, None] == starts[:, None, :], axis=2)
    last_row = jnp.any(places[None, :, None] == ends[:, None, :] - 1, axis=2)
    initial = cache.reshape(shards, REQ_DP, VALUE_HEADS, HEAD, HEAD)
    shard_rows = jnp.arange(shards, dtype=jnp.int32)

    def token_step(carry, item):
        memory, finals = carry
        query_t, key_t, value_t, beta_t, decay_t, request_t, first_t, last_t = item
        memory = jnp.where(first_t[:, None, None, None], initial[shard_rows, request_t], memory)
        recalled = jnp.einsum('dhk,dhkv->dhv', key_t, memory, precision=HIGH)
        keep = jnp.exp(decay_t)[:, :, None, None]
        write = beta_t[:, :, None, None]
        memory = keep * (memory - write * key_t[..., None] * recalled[:, :, None, :]) + write * key_t[..., None] * value_t[:, :, None, :]
        mixed = jnp.einsum('dhk,dhkv->dhv', query_t, memory, precision=HIGH)
        previous = finals[shard_rows, request_t]
        finals = finals.at[shard_rows, request_t].set(jnp.where(last_t[:, None, None, None], memory, previous))
        return ((memory, finals), mixed)

    def rows_first(array):
        return jnp.swapaxes(array, 0, 1)
    start_memory = jnp.zeros((shards, VALUE_HEADS, HEAD, HEAD), jnp.float32)
    inputs = (rows_first(query_n), rows_first(key_n), rows_first(value_f), rows_first(beta_s), rows_first(decay_s), rows_first(request), rows_first(first_row), rows_first(last_row))
    (unused, finals), mixed = lax.scan(token_step, (start_memory, initial), inputs)
    mixed = rows_first(mixed).reshape(TOKEN_ROWS_ALL, VALUE_HEADS, HEAD)
    new_states = finals.reshape(REQS, VALUE_HEADS, HEAD, HEAD)
    gate_f = gate_in.astype(jnp.float32).reshape(TOKEN_ROWS_ALL, VALUE_HEADS, HEAD)
    scale = lax.rsqrt(lax.optimization_barrier(jnp.mean(mixed * mixed, axis=-1, keepdims=True)) + epsilon)
    normed = (mixed * scale * norm_gain * jax.nn.silu(gate_f)).astype(jnp.bfloat16).reshape(TOKEN_ROWS_ALL, VALUE_HEADS * HEAD)
    attn = jnp.dot(normed, out_proj, preferred_element_type=jnp.float32)
    attn_out = (residual.astype(jnp.float32) + attn).astype(jnp.bfloat16)
    stream = attn_out.astype(jnp.float32)
    routed = (stream * lax.rsqrt(lax.optimization_barrier(jnp.mean(stream * stream, axis=-1, keepdims=True)) + epsilon) * post_gain).astype(jnp.bfloat16)
    flat_ids = expert_ids.reshape(-1).astype(jnp.int32)
    flat_weights = route_weights.reshape(-1)
    order = jnp.argsort(flat_ids, stable=True).astype(jnp.int32)
    counts = lax.optimization_barrier(jnp.sum((flat_ids[:, None] == jnp.arange(EXPERTS, dtype=jnp.int32)[None, :]).astype(jnp.int32), axis=0)).astype(jnp.int32)
    offsets = (jnp.cumsum(counts) - counts).astype(jnp.int32)
    limit = N_EXPERT * N_DP * CAP
    padded = jnp.concatenate([order, jnp.zeros((limit,), jnp.int32)])

    def expert_step(grand_count, item):
        number, weights_gu, weights_down = item
        picked = lax.dynamic_slice_in_dim(padded, offsets[number].astype(jnp.int32), limit).astype(jnp.int32)
        valid = jnp.arange(limit, dtype=jnp.int32) < counts[number]
        token_of = (picked // TOP).astype(jnp.int32)
        inputs_e = routed[token_of]
        both = jnp.dot(inputs_e, weights_gu, preferred_element_type=jnp.float32)
        hidden = (jax.nn.silu(both[:, :FF]) * both[:, FF:]).astype(jnp.bfloat16)
        result = jnp.dot(hidden, weights_down, preferred_element_type=jnp.float32).astype(jnp.bfloat16)
        weighted = jnp.where(valid[:, None], result.astype(jnp.float32) * flat_weights[picked][:, None], 0.0)
        return (grand_count.at[token_of].add(weighted), None)
    numbers = jnp.arange(EXPERTS, dtype=jnp.int32)
    grand_count, unused2 = lax.scan(expert_step, jnp.zeros((TOKEN_ROWS_ALL, D), jnp.float32), (numbers, gate_up, down_proj))
    moe_out = grand_count.astype(jnp.bfloat16)
    return (moe_out, attn_out, new_states)
```

```python
import jax
import jax.numpy as jnp
from jax import lax
from jax.sharding import PartitionSpec as P

HIGH = lax.Precision.HIGHEST
epsilon = 1e-06
block_rows = 64


def unit_rows(values):
    return values * lax.rsqrt(jnp.sum(values * values, axis=-1, keepdims=True) + epsilon)


def block_step(states, item):
    query_b, key_b, value_b, beta_b, decay_b, member_b = item
    size = query_b.shape[0]
    places = jnp.arange(size)
    shared = jnp.dot(member_b, member_b.T, precision=HIGH) > 0.5
    inside = shared & (places[:, None] >= places[None, :])
    strict_part = inside & (places[:, None] > places[None, :])
    running = jnp.dot(inside.astype(jnp.float32), decay_b, precision=HIGH).T
    log_gaps = running[:, :, None] - running[:, None, :]
    decays = jnp.where(inside[None], jnp.exp(jnp.minimum(log_gaps, 0.0)), 0.0)
    key_h = jnp.swapaxes(key_b, 0, 1)
    query_h = jnp.swapaxes(query_b, 0, 1)
    value_h = jnp.swapaxes(value_b, 0, 1)
    beta_h = beta_b.T
    key_dots = jnp.einsum("hik,hjk->hij", key_h, key_h, precision=HIGH)
    strict_terms = jnp.where(strict_part[None], decays * key_dots * beta_h[:, :, None], 0.0)
    identity = jnp.eye(size, dtype=jnp.float32)[None]
    inverse = identity - strict_terms
    powered = strict_terms
    covered = 2
    while covered < size:
        powered = jnp.einsum("hij,hjk->hik", powered, powered, precision=HIGH)
        inverse = jnp.einsum("hij,hjk->hik", inverse, identity + powered, precision=HIGH)
        covered = covered * 2
    growth = jnp.exp(running)
    targets = jnp.concatenate(
        [key_h * (beta_h * growth)[:, :, None], value_h * beta_h[:, :, None]], axis=2
    )
    solved = jnp.einsum("hij,hjc->hic", inverse, targets, precision=HIGH)
    width = key_h.shape[2]
    key_mix = solved[:, :, :width]
    value_mix = solved[:, :, width:]
    recalled = jnp.einsum("hck,hrkv->hrcv", key_mix, states, precision=HIGH)
    recalled = jnp.einsum("cr,hrcv->hcv", member_b, recalled, precision=HIGH)
    updates = value_mix - recalled
    from_state = jnp.einsum("hck,hrkv->hrcv", query_h, states, precision=HIGH)
    from_state = jnp.einsum("cr,hrcv->hcv", member_b, from_state, precision=HIGH)
    query_dots = jnp.einsum("hik,hjk->hij", query_h, key_h, precision=HIGH)
    mixed = growth[:, :, None] * from_state + jnp.einsum(
        "hij,hjv->hiv", query_dots * decays, updates, precision=HIGH
    )
    span_total = jnp.einsum("cr,ch->hr", member_b, decay_b, precision=HIGH)
    end_gaps = span_total[:, :, None] - running[:, None, :]
    carried = jnp.where(member_b.T[None] > 0.5, jnp.exp(jnp.minimum(end_gaps, 0.0)), 0.0)
    fresh = jnp.einsum("hrc,hck,hcv->hrkv", carried, key_h, updates, precision=HIGH)
    states = jnp.exp(span_total)[:, :, None, None] * states + fresh
    return (states, jnp.swapaxes(mixed, 0, 1))


def factors(size):
    low = 2 if size % 2 == 0 else 1
    return size // low, low


def partner(size, step, place):
    return place ^ step if size & (size - 1) == 0 else (place + step) % size


def source(size, step, place):
    return place ^ step if size & (size - 1) == 0 else (place - step) % size


def high_pairs(high, low, step):
    return [
        (h * low + m, partner(high, step, h) * low + m) for h in range(high) for m in range(low)
    ]


def low_pairs(high, low):
    return [(h * low + m, h * low + (m ^ 1)) for h in range(high) for m in range(low)]


def reverse(pairs):
    return [(target, origin) for origin, target in pairs]


def gather_parts(block, axis):
    high, low = factors(lax.axis_size(axis))
    parts = [[block]]
    for step in range(1, high):
        parts.append([lax.ppermute(block, axis, high_pairs(high, low, step))])
    if low == 2:
        for row in parts:
            row.append(lax.ppermute(row[0], axis, low_pairs(high, low)))
    return parts


def scatter_sum(parts, axis):
    high, low = factors(lax.axis_size(axis))
    sums = []
    for row in parts:
        total = row[0].astype(jnp.float32)
        if low == 2:
            total = total + lax.ppermute(row[1], axis, low_pairs(high, low)).astype(jnp.float32)
        sums.append(total)
    result = sums[0]
    for step in range(1, high):
        sent = sums[step].astype(jnp.bfloat16)
        result = result + lax.ppermute(
            sent, axis, reverse(high_pairs(high, low, step))
        ).astype(jnp.float32)
    return result


def part_sources(axis):
    high, low = factors(lax.axis_size(axis))
    place = lax.axis_index(axis)
    h, m = place // low, place % low
    return [[source(high, step, h) * low + (m ^ j) for j in range(low)] for step in range(high)]


def on_device(
    queries,
    keys_in,
    values_in,
    gate_in,
    beta,
    decay,
    lengths,
    cache,
    norm_gain,
    out_proj,
    residual,
    post_gain,
    expert_ids,
    route_weights,
    gate_up,
    down_proj,
):
    tok_count = queries.shape[0]
    heads = beta.shape[1]
    head_dim = norm_gain.shape[0]
    requests = lengths.shape[1]
    block = min(block_rows, tok_count)
    blocks = tok_count // block
    layout = (blocks, block, heads, head_dim)
    query_n = unit_rows(queries.astype(jnp.float32).reshape(layout)) * head_dim ** (-0.5)
    key_n = unit_rows(keys_in.astype(jnp.float32).reshape(layout))
    value_f = values_in.astype(jnp.float32).reshape(layout)
    ends = jnp.cumsum(lengths[0])
    places = jnp.arange(tok_count, dtype=jnp.int32)
    request = jnp.sum((places[:, None] >= ends[None, :]).astype(jnp.int32), axis=1)
    member = (request[:, None] == jnp.arange(requests, dtype=jnp.int32)[None, :]).astype(
        jnp.float32
    )
    inputs = (
        query_n,
        key_n,
        value_f,
        beta.reshape(blocks, block, heads),
        decay.reshape(blocks, block, heads),
        member.reshape(blocks, block, requests),
    )
    states, mixed = lax.scan(block_step, jnp.swapaxes(cache, 0, 1), inputs)
    new_states = jnp.swapaxes(states, 0, 1)
    mixed = mixed.reshape(tok_count, heads, head_dim)
    gate_f = gate_in.astype(jnp.float32).reshape(tok_count, heads, head_dim)
    scale = lax.rsqrt(jnp.mean(mixed * mixed, axis=-1, keepdims=True) + epsilon)
    normed = (
        (mixed * scale * norm_gain * jax.nn.silu(gate_f))
        .astype(jnp.bfloat16)
        .reshape(tok_count, heads * head_dim)
    )
    width = residual.shape[1]
    tok_local = residual.shape[0]
    experts_all = lax.axis_size("expert") * lax.axis_size("dp")
    gate_up_parts = sum(gather_parts(gate_up[0], "dp"), [])
    down_parts = sum(gather_parts(down_proj[0], "dp"), [])
    expert_of = sum(part_sources("dp"), [])
    expert_of = [lax.axis_index("expert") * lax.axis_size("dp") + place for place in expert_of]
    share = jnp.dot(normed, out_proj, preferred_element_type=jnp.float32).astype(jnp.bfloat16)
    share = share.reshape(lax.axis_size("expert"), tok_local, width)
    attn = scatter_sum(
        [
            [lax.dynamic_index_in_dim(share, place, 0, keepdims=False) for place in row]
            for row in part_sources("expert")
        ],
        "expert",
    )
    attn_out = (residual.astype(jnp.float32) + attn).astype(jnp.bfloat16)
    stream = attn_out.astype(jnp.float32)
    routed = (
        stream * lax.rsqrt(jnp.mean(stream * stream, axis=-1, keepdims=True) + epsilon) * post_gain
    ).astype(jnp.bfloat16)
    expert_range = jnp.arange(experts_all, dtype=jnp.int32)
    mixing = jnp.sum(
        jnp.where(expert_ids[:, :, None] == expert_range, route_weights[:, :, None], 0.0), axis=1
    )
    coarse = mixing.astype(jnp.bfloat16)
    fine = (mixing - coarse.astype(jnp.float32)).astype(jnp.bfloat16)
    gathered = gather_parts(jnp.concatenate([routed, coarse, fine], axis=1), "expert")
    rows = jnp.concatenate(sum(gathered, []), axis=0)
    weights = rows[:, width : width + experts_all].astype(jnp.float32) + rows[
        :, width + experts_all :
    ].astype(jnp.float32)
    rows = rows[:, :width]
    hidden_width = down_proj.shape[1]
    hidden = []
    for place, matrix in zip(expert_of, gate_up_parts):
        weight = jnp.sum(jnp.where(expert_range == place, weights, 0.0), axis=1, keepdims=True)
        both = jnp.dot(rows, matrix, preferred_element_type=jnp.float32)
        hidden.append(
            (weight * jax.nn.silu(both[:, :hidden_width]) * both[:, hidden_width:]).astype(
                jnp.bfloat16
            )
        )
    result = jnp.dot(
        jnp.concatenate(hidden, axis=1),
        jnp.concatenate(down_parts, axis=0),
        preferred_element_type=jnp.float32,
    ).astype(jnp.bfloat16)
    high, low = factors(lax.axis_size("expert"))
    result = result.reshape(high, low, tok_local, width)
    moe_out = scatter_sum(
        [[result[step, j] for j in range(low)] for step in range(high)], "expert"
    ).astype(jnp.bfloat16)
    return (moe_out, attn_out, new_states)


def solution(mesh):
    return jax.shard_map(
        on_device,
        mesh=mesh,
        in_specs=(
            P(("groups", "dp"), "expert"),
            P(("groups", "dp"), "expert"),
            P(("groups", "dp"), "expert"),
            P(("groups", "dp"), "expert"),
            P(("groups", "dp"), "expert"),
            P(("groups", "dp"), "expert"),
            P(("groups", "dp"), None),
            P(("groups", "dp"), "expert", None, None),
            P(),
            P("expert", None),
            P(("groups", "dp", "expert"), None),
            P(),
            P(("groups", "dp", "expert"), None),
            P(("groups", "dp", "expert"), None),
            P(("expert", "dp"), None, None),
            P(("expert", "dp"), None, None),
        ),
        out_specs=(
            P(("groups", "dp", "expert"), None),
            P(("groups", "dp", "expert"), None),
            P(("groups", "dp"), "expert", None, None),
        ),
        check_vma=False,
    )
```

```python
import functools

import jax
import jax.numpy as jnp
from jax import lax
from jax.experimental import pallas as pl
from jax.experimental.pallas import tpu as pltpu
from jax.sharding import PartitionSpec as P


HIGH = lax.Precision.HIGHEST
epsilon = 1e-06
chunk_rows = 128


def product(left, right, contract=((1,), (0,))):
    left, right = left.astype(jnp.bfloat16), right.astype(jnp.bfloat16)
    return lax.dot_general(left, right, (contract, ((), ())), preferred_element_type=jnp.float32)


def mix_kernel(
    heads,
    requests,
    query_ref,
    key_ref,
    value_ref,
    gate_ref,
    beta_ref,
    decay_ref,
    lengths_ref,
    cache_ref,
    gain_ref,
    proj_ref,
    share_ref,
    states_ref,
):
    step = pl.program_id(0)
    rows = query_ref.shape[0]
    dim = gain_ref.shape[1]
    f32, bf16 = jnp.float32, jnp.bfloat16

    @pl.when(step == 0)
    def _():
        states_ref[...] = cache_ref[...]

    row_of = lax.broadcasted_iota(jnp.int32, (rows, rows), 0)
    col_of = lax.broadcasted_iota(jnp.int32, (rows, rows), 1)
    request_col = jnp.zeros((rows, 1), jnp.int32)
    request_row = jnp.zeros((1, rows), jnp.int32)
    place_col = lax.broadcasted_iota(jnp.int32, (rows, 1), 0) + step * rows
    place_row = lax.broadcasted_iota(jnp.int32, (1, rows), 1) + step * rows
    end = jnp.int32(0)
    for r in range(requests):
        end = end + lengths_ref[0, r]
        request_col = request_col + (place_col >= end).astype(jnp.int32)
        request_row = request_row + (place_row >= end).astype(jnp.int32)
    shared = request_col == request_row
    inside = shared & (row_of >= col_of)
    after = shared & (row_of < col_of)
    strict = shared & (row_of > col_of)
    eye = (row_of == col_of).astype(f32)
    decay = decay_ref[...]
    inside_f = inside.astype(f32)
    running = lax.dot_general(
        inside_f, decay, (((1,), (0,)), ((), ())), precision=HIGH, preferred_element_type=f32
    )
    running_t = lax.dot_general(
        decay, inside_f, (((0,), (1,)), ((), ())), precision=HIGH, preferred_element_type=f32
    )
    left = lax.dot_general(
        after.astype(f32), decay, (((1,), (0,)), ((), ())), precision=HIGH, preferred_element_type=f32
    )
    totals = [
        jnp.exp(jnp.sum(jnp.where(request_col == r, decay, 0.0), axis=0, keepdims=True))
        for r in range(requests)
    ]
    in_col = [request_col == r for r in range(requests)]
    in_row = [request_row == r for r in range(requests)]
    levels = []
    span = 2
    while span < rows:
        levels.append(
            (row_of // (2 * span) == col_of // (2 * span))
            & ((row_of // span) % 2 == 1)
            & ((col_of // span) % 2 == 0)
        )
        span *= 2
    first = (row_of // 2 == col_of // 2) & (row_of != col_of)

    keys, queries, betas, growths, dots_q, terms, inverses = [], [], [], [], [], [], []
    for h in range(heads):
        lanes = slice(h * dim, (h + 1) * dim)
        key = key_ref[:, lanes].astype(f32)
        key = key * lax.rsqrt(jnp.sum(key * key, axis=-1, keepdims=True) + epsilon)
        query = query_ref[:, lanes].astype(f32)
        query = query * (
            lax.rsqrt(jnp.sum(query * query, axis=-1, keepdims=True) + epsilon) * dim ** (-0.5)
        )
        beta = beta_ref[:, h : h + 1]
        gaps = running[:, h : h + 1] - running_t[h : h + 1, :]
        decays = jnp.where(inside, jnp.exp(jnp.minimum(gaps, 0.0)), 0.0)
        key_b = key.astype(bf16)
        both = product(
            jnp.concatenate([key_b, query.astype(bf16)], axis=0), key_b, ((1,), (1,))
        )
        terms.append(jnp.where(strict, decays * both[:rows] * beta, 0.0))
        dots_q.append((both[rows:] * decays).astype(bf16))
        keys.append(key)
        queries.append(query)
        betas.append(beta)
        growths.append(jnp.exp(running[:, h : h + 1]))
    inverses = [eye - jnp.where(first, term, 0.0) for term in terms]
    for mask in levels:
        inner = [
            product(jnp.where(mask, terms[h], 0.0), inverses[h]) for h in range(heads)
        ]
        inverses = [
            inverses[h] - product(inverses[h], inner[h]) for h in range(heads)
        ]
    normed = []
    for h in range(heads):
        lanes = slice(h * dim, (h + 1) * dim)
        targets = jnp.concatenate(
            [keys[h] * (betas[h] * growths[h]), value_ref[:, lanes].astype(f32) * betas[h]], axis=1
        )
        solved = product(inverses[h], targets)
        probe = jnp.concatenate(
            [solved[:, :dim].astype(bf16), (queries[h] * growths[h]).astype(bf16)], axis=0
        )
        wide = jnp.concatenate(
            [jnp.where(jnp.concatenate([in_col[r], in_col[r]], axis=0), probe, 0) for r in range(requests)],
            axis=1,
        )
        state = states_ref[:, h].reshape(requests * dim, dim)
        seen = product(wide, state)
        update = (solved[:, dim:] - seen[:rows]).astype(bf16)
        mixed = seen[rows:] + product(dots_q[h], update)
        key_t = (keys[h] * jnp.exp(left[:, h : h + 1])).T.astype(bf16)
        for r in range(requests):
            fresh = product(jnp.where(in_row[r], key_t, 0), update)
            states_ref[r, h] = totals[r][:, h : h + 1] * states_ref[r, h] + fresh
        scale = lax.rsqrt(jnp.mean(mixed * mixed, axis=-1, keepdims=True) + epsilon)
        gate = gate_ref[:, lanes].astype(f32)
        normed.append(
            (mixed * scale * gain_ref[...] * (gate * jax.nn.sigmoid(gate))).astype(bf16)
        )
    share_ref[...] = product(jnp.concatenate(normed, axis=1), proj_ref[...]).astype(bf16)


def mix(queries, keys_in, values_in, gate_in, beta, decay, lengths, cache, norm_gain, out_proj):
    tok_count, heads = beta.shape
    requests = lengths.shape[1]
    dim = norm_gain.shape[0]
    rows = min(chunk_rows, tok_count)
    width = out_proj.shape[1]
    block = lambda cols: pl.BlockSpec((rows, cols), lambda c: (c, 0))
    whole = lambda shape: pl.BlockSpec(shape, lambda c: (0,) * len(shape))
    return pl.pallas_call(
        functools.partial(mix_kernel, heads, requests),
        grid=(tok_count // rows,),
        in_specs=[
            block(heads * dim),
            block(heads * dim),
            block(heads * dim),
            block(heads * dim),
            block(heads),
            block(heads),
            pl.BlockSpec(memory_space=pltpu.SMEM),
            whole(cache.shape),
            whole((1, dim)),
            whole(out_proj.shape),
        ],
        out_specs=[block(width), whole(cache.shape)],
        out_shape=[
            jax.ShapeDtypeStruct((tok_count, width), jnp.bfloat16),
            jax.ShapeDtypeStruct(cache.shape, jnp.float32),
        ],
        compiler_params=pltpu.CompilerParams(dimension_semantics=("arbitrary",)),
        name="mix",
    )(queries, keys_in, values_in, gate_in, beta, decay, lengths, cache, norm_gain[None], out_proj)


def factors(size):
    low = 2 if size % 2 == 0 else 1
    return size // low, low


def partner(size, step, place):
    return place ^ step if size & (size - 1) == 0 else (place + step) % size


def source(size, step, place):
    return place ^ step if size & (size - 1) == 0 else (place - step) % size


def high_pairs(high, low, step):
    return [
        (h * low + m, partner(high, step, h) * low + m) for h in range(high) for m in range(low)
    ]


def low_pairs(high, low):
    return [(h * low + m, h * low + (m ^ 1)) for h in range(high) for m in range(low)]


def reverse(pairs):
    return [(target, origin) for origin, target in pairs]


def gather_parts(block, axis):
    high, low = factors(lax.axis_size(axis))
    parts = [[block]]
    for step in range(1, high):
        parts.append([lax.ppermute(block, axis, high_pairs(high, low, step))])
    if low == 2:
        for row in parts:
            row.append(lax.ppermute(row[0], axis, low_pairs(high, low)))
    return parts


def scatter_sum(parts, axis):
    high, low = factors(lax.axis_size(axis))
    sums = []
    for row in parts:
        total = row[0].astype(jnp.float32)
        if low == 2:
            total = total + lax.ppermute(row[1], axis, low_pairs(high, low)).astype(jnp.float32)
        sums.append(total)
    result = sums[0]
    for step in range(1, high):
        sent = sums[step].astype(jnp.bfloat16)
        result = result + lax.ppermute(
            sent, axis, reverse(high_pairs(high, low, step))
        ).astype(jnp.float32)
    return result


def part_sources(axis):
    high, low = factors(lax.axis_size(axis))
    place = lax.axis_index(axis)
    h, m = place // low, place % low
    return [[source(high, step, h) * low + (m ^ j) for j in range(low)] for step in range(high)]


def on_device(
    queries,
    keys_in,
    values_in,
    gate_in,
    beta,
    decay,
    lengths,
    cache,
    norm_gain,
    out_proj,
    residual,
    post_gain,
    expert_ids,
    route_weights,
    gate_up,
    down_proj,
):
    width = residual.shape[1]
    tok_local = residual.shape[0]
    experts_all = lax.axis_size("expert") * lax.axis_size("dp")
    gate_up_parts = sum(gather_parts(gate_up[0], "dp"), [])
    down_parts = sum(gather_parts(down_proj[0], "dp"), [])
    expert_of = sum(part_sources("dp"), [])
    expert_of = [lax.axis_index("expert") * lax.axis_size("dp") + place for place in expert_of]
    share, new_states = mix(
        queries,
        keys_in,
        values_in,
        gate_in,
        beta,
        decay,
        lengths,
        cache,
        norm_gain,
        out_proj,
    )
    share = share.reshape(lax.axis_size("expert"), tok_local, width)
    attn = scatter_sum(
        [
            [lax.dynamic_index_in_dim(share, place, 0, keepdims=False) for place in row]
            for row in part_sources("expert")
        ],
        "expert",
    )
    attn_out = (residual.astype(jnp.float32) + attn).astype(jnp.bfloat16)
    stream = attn_out.astype(jnp.float32)
    routed = (
        stream * lax.rsqrt(jnp.mean(stream * stream, axis=-1, keepdims=True) + epsilon) * post_gain
    ).astype(jnp.bfloat16)
    expert_range = jnp.arange(experts_all, dtype=jnp.int32)
    mixing = jnp.sum(
        jnp.where(expert_ids[:, :, None] == expert_range, route_weights[:, :, None], 0.0), axis=1
    )
    coarse = mixing.astype(jnp.bfloat16)
    fine = (mixing - coarse.astype(jnp.float32)).astype(jnp.bfloat16)
    gathered = gather_parts(jnp.concatenate([routed, coarse, fine], axis=1), "expert")
    rows = jnp.concatenate(sum(gathered, []), axis=0)
    weights = rows[:, width : width + experts_all].astype(jnp.float32) + rows[
        :, width + experts_all :
    ].astype(jnp.float32)
    rows = rows[:, :width]
    hidden_width = down_proj.shape[1]
    hidden = []
    for place, matrix in zip(expert_of, gate_up_parts):
        weight = jnp.sum(jnp.where(expert_range == place, weights, 0.0), axis=1, keepdims=True)
        both = jnp.dot(rows, matrix, preferred_element_type=jnp.float32)
        hidden.append(
            (weight * jax.nn.silu(both[:, :hidden_width]) * both[:, hidden_width:]).astype(
                jnp.bfloat16
            )
        )
    result = jnp.dot(
        jnp.concatenate(hidden, axis=1),
        jnp.concatenate(down_parts, axis=0),
        preferred_element_type=jnp.float32,
    ).astype(jnp.bfloat16)
    high, low = factors(lax.axis_size("expert"))
    result = result.reshape(high, low, tok_local, width)
    moe_out = scatter_sum(
        [[result[step, j] for j in range(low)] for step in range(high)], "expert"
    ).astype(jnp.bfloat16)
    return (moe_out, attn_out, new_states)


def solution(mesh):
    return jax.shard_map(
        on_device,
        mesh=mesh,
        in_specs=(
            P(("groups", "dp"), "expert"),
            P(("groups", "dp"), "expert"),
            P(("groups", "dp"), "expert"),
            P(("groups", "dp"), "expert"),
            P(("groups", "dp"), "expert"),
            P(("groups", "dp"), "expert"),
            P(("groups", "dp"), None),
            P(("groups", "dp"), "expert", None, None),
            P(),
            P("expert", None),
            P(("groups", "dp", "expert"), None),
            P(),
            P(("groups", "dp", "expert"), None),
            P(("groups", "dp", "expert"), None),
            P(("expert", "dp"), None, None),
            P(("expert", "dp"), None, None),
        ),
        out_specs=(
            P(("groups", "dp", "expert"), None),
            P(("groups", "dp", "expert"), None),
            P(("groups", "dp"), "expert", None, None),
        ),
        check_vma=False,
    )
```

```python
import functools

import jax
import jax.numpy as jnp
from jax import lax
from jax.experimental import pallas as pl
from jax.experimental.pallas import tpu as pltpu
from jax.sharding import PartitionSpec as P


HIGH = lax.Precision.HIGHEST
epsilon = 1e-06
chunk_rows = 128


def product(left, right, contract=((1,), (0,))):
    left, right = left.astype(jnp.bfloat16), right.astype(jnp.bfloat16)
    return lax.dot_general(left, right, (contract, ((), ())), preferred_element_type=jnp.float32)


def exact_product(left, right):
    return lax.dot_general(
        left, right, (((1,), (1,)), ((), ())), precision=HIGH, preferred_element_type=jnp.float32
    )


def mix_kernel(
    heads,
    requests,
    owned,
    query_ref,
    key_ref,
    value_ref,
    gate_ref,
    beta_ref,
    decay_ref,
    lengths_ref,
    cache_ref,
    gain_ref,
    proj_ref,
    share_ref,
    states_ref,
):
    step = pl.program_id(0)
    rows = query_ref.shape[0]
    dim = gain_ref.shape[1]
    f32, bf16 = jnp.float32, jnp.bfloat16

    @pl.when(step == 0)
    def _():
        states_ref[...] = cache_ref[...]

    row_of = lax.broadcasted_iota(jnp.int32, (rows, rows), 0)
    col_of = lax.broadcasted_iota(jnp.int32, (rows, rows), 1)
    request_col = jnp.zeros((rows, 1), jnp.int32)
    request_row = jnp.zeros((1, rows), jnp.int32)
    place_col = lax.broadcasted_iota(jnp.int32, (rows, 1), 0) + step * rows
    place_row = lax.broadcasted_iota(jnp.int32, (1, rows), 1) + step * rows
    end = jnp.int32(0)
    for r in range(requests):
        end = end + lengths_ref[0, r]
        request_col = request_col + (place_col >= end).astype(jnp.int32)
        request_row = request_row + (place_row >= end).astype(jnp.int32)
    shared = request_col == request_row
    inside = shared & (row_of >= col_of)
    after = shared & (row_of < col_of)
    strict = shared & (row_of > col_of)
    eye = (row_of == col_of).astype(f32)
    decay = decay_ref[...]
    inside_f = inside.astype(f32)
    running = exact_product(inside_f, decay)
    running_t = exact_product(decay, inside_f)
    left = exact_product(after.astype(f32), decay)
    strength = exact_product(eye, beta_ref[...])
    totals = [
        jnp.exp(jnp.sum(jnp.where(request_row == r, decay, 0.0), axis=1, keepdims=True))
        for r in range(requests)
    ]
    in_col = [request_col == r for r in range(requests)]
    in_row = [request_row == r for r in range(requests)]
    levels = []
    span = 2
    while span < rows:
        levels.append(
            (row_of // (2 * span) == col_of // (2 * span))
            & ((row_of // span) % 2 == 1)
            & ((col_of // span) % 2 == 0)
        )
        span *= 2
    first = (row_of // 2 == col_of // 2) & (row_of != col_of)

    keys, queries, betas, growths, dots_q, terms, inverses = [], [], [], [], [], [], []
    for h in range(heads):
        lanes = slice(h * dim, (h + 1) * dim)
        key = key_ref[:, lanes].astype(f32)
        key = key * lax.rsqrt(jnp.sum(key * key, axis=-1, keepdims=True) + epsilon)
        query = query_ref[:, lanes].astype(f32)
        query = query * (
            lax.rsqrt(jnp.sum(query * query, axis=-1, keepdims=True) + epsilon) * dim ** (-0.5)
        )
        beta = strength[:, h : h + 1]
        gaps = running[:, h : h + 1] - running_t[h : h + 1, :]
        decays = jnp.where(inside, jnp.exp(jnp.minimum(gaps, 0.0)), 0.0)
        key_b = key.astype(bf16)
        both = product(
            jnp.concatenate([key_b, query.astype(bf16)], axis=0), key_b, ((1,), (1,))
        )
        terms.append(jnp.where(strict, decays * both[:rows] * beta, 0.0))
        dots_q.append((both[rows:] * decays).astype(bf16))
        keys.append(key)
        queries.append(query)
        betas.append(beta)
        growths.append(jnp.exp(running[:, h : h + 1]))
    inverses = [eye - jnp.where(first, term, 0.0) for term in terms]
    for mask in levels:
        inner = [
            product(jnp.where(mask, terms[h], 0.0), inverses[h]) for h in range(heads)
        ]
        inverses = [
            inverses[h] - product(inverses[h], inner[h]) for h in range(heads)
        ]
    normed = []
    for h in range(heads):
        lanes = slice(h * dim, (h + 1) * dim)
        targets = jnp.concatenate(
            [keys[h] * (betas[h] * growths[h]), value_ref[:, lanes].astype(f32) * betas[h]], axis=1
        )
        solved = product(inverses[h], targets)
        probe = jnp.concatenate(
            [solved[:, :dim].astype(bf16), (queries[h] * growths[h]).astype(bf16)], axis=0
        )
        wide = jnp.concatenate(
            [jnp.where(jnp.concatenate([in_col[r], in_col[r]], axis=0), probe, 0) for r in range(requests)],
            axis=1,
        )
        state = states_ref[:, h].reshape(requests * dim, dim)
        seen = product(wide, state)
        update = (solved[:, dim:] - seen[:rows]).astype(bf16)
        mixed = seen[rows:] + product(dots_q[h], update)
        key_t = (keys[h] * jnp.exp(left[:, h : h + 1])).T.astype(bf16)
        for r in range(requests):
            fresh = product(jnp.where(in_row[r], key_t, 0), update)
            states_ref[r, h] = totals[r][h : h + 1, :] * states_ref[r, h] + fresh
        scale = lax.rsqrt(jnp.mean(mixed * mixed, axis=-1, keepdims=True) + epsilon)
        gate = gate_ref[:, lanes].astype(f32)
        normed.append(
            (mixed * scale * gain_ref[...] * (gate * jax.nn.sigmoid(gate))).astype(bf16)
        )
    share = product(jnp.concatenate(normed, axis=1), proj_ref[...]).astype(bf16)
    for block in range(rows // owned):
        slot = part_slot("expert", step * (rows // owned) + block)
        share_ref[pl.ds(pl.multiple_of(slot * owned, owned), owned), :] = share[
            block * owned : (block + 1) * owned
        ]


def mix(queries, keys_in, values_in, gate_in, beta, decay, lengths, cache, norm_gain, out_proj, owned):
    tok_count, heads = beta.shape
    requests = lengths.shape[1]
    dim = norm_gain.shape[0]
    rows = min(chunk_rows, tok_count)
    width = out_proj.shape[1]
    block = lambda cols: pl.BlockSpec((rows, cols), lambda c: (c, 0))
    whole = lambda shape: pl.BlockSpec(shape, lambda c: (0,) * len(shape))
    return pl.pallas_call(
        functools.partial(mix_kernel, heads, requests, owned),
        grid=(tok_count // rows,),
        in_specs=[
            block(heads * dim),
            block(heads * dim),
            block(heads * dim),
            block(heads * dim),
            pl.BlockSpec((heads, rows), lambda c: (0, c)),
            pl.BlockSpec((heads, rows), lambda c: (0, c)),
            pl.BlockSpec(memory_space=pltpu.SMEM),
            whole(cache.shape),
            whole((1, dim)),
            whole(out_proj.shape),
        ],
        out_specs=[whole((tok_count, width)), whole(cache.shape)],
        out_shape=[
            jax.ShapeDtypeStruct((tok_count, width), jnp.bfloat16),
            jax.ShapeDtypeStruct(cache.shape, jnp.float32),
        ],
        compiler_params=pltpu.CompilerParams(dimension_semantics=("arbitrary",)),
        name="mix",
    )(
        queries,
        keys_in,
        values_in,
        gate_in,
        beta.T,
        decay.T,
        lengths,
        cache,
        norm_gain[None],
        out_proj,
    )


def factors(size):
    low = 2 if size % 2 == 0 else 1
    return size // low, low


def partner(size, step, place):
    return place ^ step if size & (size - 1) == 0 else (place + step) % size


def source(size, step, place):
    return place ^ step if size & (size - 1) == 0 else (place - step) % size


def high_pairs(high, low, step):
    return [
        (h * low + m, partner(high, step, h) * low + m) for h in range(high) for m in range(low)
    ]


def low_pairs(high, low):
    return [(h * low + m, h * low + (m ^ 1)) for h in range(high) for m in range(low)]


def reverse(pairs):
    return [(target, origin) for origin, target in pairs]


def gather_parts(block, axis):
    high, low = factors(lax.axis_size(axis))
    parts = [[block]]
    for step in range(1, high):
        parts.append([lax.ppermute(block, axis, high_pairs(high, low, step))])
    if low == 2:
        for row in parts:
            row.append(lax.ppermute(row[0], axis, low_pairs(high, low)))
    return parts


def scatter_sum(parts, axis):
    high, low = factors(lax.axis_size(axis))
    order = list(range(high - 1, 0, -1)) + [0]
    near = {}
    if low == 2:
        for step in order:
            near[step] = lax.ppermute(parts[step][1], axis, low_pairs(high, low))
    sums, before = {}, None
    for step in order:
        total = parts[step][0].astype(jnp.float32)
        if low == 2:
            other = near[step]
            if before is not None:
                other, before = lax.optimization_barrier((other, before))
            total = total + other.astype(jnp.float32)
        if step:
            before = total.astype(jnp.bfloat16)
            sums[step] = lax.ppermute(before, axis, reverse(high_pairs(high, low, step)))
    for step in order[:-1]:
        total = total + sums[step].astype(jnp.float32)
    return total


def part_slot(axis, owner):
    high, low = factors(lax.axis_size(axis))
    place = lax.axis_index(axis)
    h, m = place // low, place % low
    other, n = owner // low, owner % low
    step = other ^ h if high & (high - 1) == 0 else (h - other + high) % high
    return step * low + (m ^ n)


def part_sources(axis):
    high, low = factors(lax.axis_size(axis))
    place = lax.axis_index(axis)
    h, m = place // low, place % low
    return [[source(high, step, h) * low + (m ^ j) for j in range(low)] for step in range(high)]


def on_device(
    queries,
    keys_in,
    values_in,
    gate_in,
    beta,
    decay,
    lengths,
    cache,
    norm_gain,
    out_proj,
    residual,
    post_gain,
    expert_ids,
    route_weights,
    gate_up,
    down_proj,
):
    width = residual.shape[1]
    tok_local = residual.shape[0]
    experts_all = lax.axis_size("expert") * lax.axis_size("dp")
    gate_up_parts = sum(gather_parts(gate_up[0], "dp"), [])
    down_parts = sum(gather_parts(down_proj[0], "dp"), [])
    expert_of = sum(part_sources("dp"), [])
    expert_of = [lax.axis_index("expert") * lax.axis_size("dp") + place for place in expert_of]
    share, new_states = mix(
        queries,
        keys_in,
        values_in,
        gate_in,
        beta,
        decay,
        lengths,
        cache,
        norm_gain,
        out_proj,
        tok_local,
    )
    high, low = factors(lax.axis_size("expert"))
    share = share.reshape(high, low, tok_local, width)
    attn = scatter_sum([[share[step, j] for j in range(low)] for step in range(high)], "expert")
    attn_out = (residual.astype(jnp.float32) + attn).astype(jnp.bfloat16)
    stream = attn_out.astype(jnp.float32)
    routed = (
        stream * lax.rsqrt(jnp.mean(stream * stream, axis=-1, keepdims=True) + epsilon) * post_gain
    ).astype(jnp.bfloat16)
    expert_range = jnp.arange(experts_all, dtype=jnp.int32)
    mixing = jnp.sum(
        jnp.where(expert_ids[:, :, None] == expert_range, route_weights[:, :, None], 0.0), axis=1
    )
    coarse = mixing.astype(jnp.bfloat16)
    fine = (mixing - coarse.astype(jnp.float32)).astype(jnp.bfloat16)
    pad = jnp.zeros((tok_local, -2 * experts_all % 128), jnp.bfloat16)
    gathered = gather_parts(jnp.concatenate([routed, coarse, fine, pad], axis=1), "expert")
    places = jnp.stack(expert_of).astype(jnp.int32)
    split = max(1, high // 2)
    results = []
    for first in range(0, high, split):
        results += experts(
            places,
            sum(gathered[first : first + split], []),
            gate_up_parts,
            down_parts,
            experts_all,
        )
    moe_out = scatter_sum(
        [results[step * low : (step + 1) * low] for step in range(high)], "expert"
    ).astype(jnp.bfloat16)
    return (moe_out, attn_out, new_states)


def experts_kernel(blocks, slots, experts_all, places_ref, *refs):
    row_refs = refs[:blocks]
    gate_up_refs = refs[blocks : blocks + slots]
    down_refs = refs[blocks + slots : blocks + 2 * slots]
    out_refs = refs[blocks + 2 * slots : 2 * blocks + 2 * slots]
    gate_up_buf, down_buf, hidden_buf, gate_up_sem, down_sem = refs[2 * blocks + 2 * slots :]
    width, hidden_width = gate_up_buf.shape[1], down_buf.shape[1]
    loads = [
        pltpu.make_async_copy(gate_up_refs[i], gate_up_buf.at[i], gate_up_sem.at[i])
        for i in range(slots)
    ]
    loads_down = [
        pltpu.make_async_copy(down_refs[i], down_buf.at[i], down_sem.at[i]) for i in range(slots)
    ]
    for load in loads + loads_down:
        load.start()
    rows = jnp.concatenate([ref[:, :width] for ref in row_refs], axis=0)
    mixing = jnp.concatenate([ref[:, width:] for ref in row_refs], axis=0).astype(jnp.float32)
    lane = lax.broadcasted_iota(jnp.int32, mixing.shape, 1)
    for i in range(slots):
        place = places_ref[i]
        named = (lane == place) | (lane == place + experts_all)
        weight = jnp.sum(jnp.where(named, mixing, 0.0), axis=1, keepdims=True)
        loads[i].wait()
        both = product(rows, gate_up_buf[i])
        gate = both[:, :hidden_width]
        hidden = gate * jax.nn.sigmoid(gate) * both[:, hidden_width:] * weight
        hidden_buf[:, i * hidden_width : (i + 1) * hidden_width] = hidden.astype(jnp.bfloat16)
    for load in loads_down:
        load.wait()
    size = row_refs[0].shape[0]
    tile = min(512, width)
    for start in range(0, width, tile):
        down = jnp.concatenate([down_buf[i, :, start : start + tile] for i in range(slots)], axis=0)
        result = product(hidden_buf[...], down).astype(jnp.bfloat16)
        for n in range(blocks):
            out_refs[n][:, start : start + tile] = result[n * size : (n + 1) * size]


def experts(places, row_blocks, gate_up_parts, down_parts, experts_all):
    blocks, slots = len(row_blocks), len(gate_up_parts)
    size = row_blocks[0].shape[0]
    width, hidden_twice = gate_up_parts[0].shape
    hidden_width = down_parts[0].shape[0]
    vmem = pl.BlockSpec(memory_space=pltpu.VMEM)
    return pl.pallas_call(
        functools.partial(experts_kernel, blocks, slots, experts_all),
        in_specs=[pl.BlockSpec(memory_space=pltpu.SMEM)]
        + [vmem] * blocks
        + [pl.BlockSpec(memory_space=pl.ANY)] * (2 * slots),
        out_specs=[vmem] * blocks,
        out_shape=[jax.ShapeDtypeStruct((size, width), jnp.bfloat16)] * blocks,
        scratch_shapes=[
            pltpu.VMEM((slots, width, hidden_twice), jnp.bfloat16),
            pltpu.VMEM((slots, hidden_width, width), jnp.bfloat16),
            pltpu.VMEM((blocks * size, slots * hidden_width), jnp.bfloat16),
            pltpu.SemaphoreType.DMA((slots,)),
            pltpu.SemaphoreType.DMA((slots,)),
        ],
        cost_estimate=pl.CostEstimate(
            flops=2 * blocks * size * slots * width * (hidden_twice + hidden_width),
            bytes_accessed=2 * slots * width * (hidden_twice + hidden_width),
            transcendentals=0,
        ),
        name="experts",
    )(places, *row_blocks, *gate_up_parts, *down_parts)


def solution(mesh):
    return jax.shard_map(
        on_device,
        mesh=mesh,
        in_specs=(
            P(("groups", "dp"), "expert"),
            P(("groups", "dp"), "expert"),
            P(("groups", "dp"), "expert"),
            P(("groups", "dp"), "expert"),
            P(("groups", "dp"), "expert"),
            P(("groups", "dp"), "expert"),
            P(("groups", "dp"), None),
            P(("groups", "dp"), "expert", None, None),
            P(),
            P("expert", None),
            P(("groups", "dp", "expert"), None),
            P(),
            P(("groups", "dp", "expert"), None),
            P(("groups", "dp", "expert"), None),
            P(("expert", "dp"), None, None),
            P(("expert", "dp"), None, None),
        ),
        out_specs=(
            P(("groups", "dp", "expert"), None),
            P(("groups", "dp", "expert"), None),
            P(("groups", "dp"), "expert", None, None),
        ),
        check_vma=False,
    )
```

```python
import functools

import jax
import jax.numpy as jnp
from jax import lax
from jax.experimental import pallas as pl
from jax.experimental.pallas import tpu as pltpu
from jax.sharding import PartitionSpec as P


epsilon = 1e-06
chunk_rows = 128
chunks_per_step = 2


def product(left, right, contract=((1,), (0,))):
    left, right = left.astype(jnp.bfloat16), right.astype(jnp.bfloat16)
    return lax.dot_general(left, right, (contract, ((), ())), preferred_element_type=jnp.float32)


def split_exact(value):
    parts = []
    for _ in range(3):
        part = value.astype(jnp.bfloat16)
        parts.append(part)
        value = value - part.astype(jnp.float32)
    return jnp.concatenate(parts, axis=0)


def mix_kernel(
    heads,
    requests,
    owned,
    rows,
    query_ref,
    key_ref,
    value_ref,
    gate_ref,
    beta_ref,
    decay_ref,
    lengths_ref,
    cache_ref,
    gain_ref,
    proj_ref,
    states_ref,
    *share_refs,
):
    step = pl.program_id(0)
    parts = query_ref.shape[0] // rows
    dim = gain_ref.shape[1]
    f32, bf16 = jnp.float32, jnp.bfloat16

    @pl.when(step == 0)
    def _():
        states_ref[...] = cache_ref[...]

    row_of = lax.broadcasted_iota(jnp.int32, (rows, rows), 0)
    col_of = lax.broadcasted_iota(jnp.int32, (rows, rows), 1)
    eye = (row_of == col_of).astype(f32)
    levels = []
    span = 2
    while span < rows:
        levels.append(
            (row_of // (2 * span) == col_of // (2 * span))
            & ((row_of // span) % 2 == 1)
            & ((col_of // span) % 2 == 0)
        )
        span *= 2
    first = (row_of // 2 == col_of // 2) & (row_of != col_of)

    chunks, terms = [], []
    for part in range(parts):
        here = slice(part * rows, (part + 1) * rows)
        request_col = jnp.zeros((rows, 1), jnp.int32)
        request_row = jnp.zeros((1, rows), jnp.int32)
        base = (step * parts + part) * rows
        place_col = lax.broadcasted_iota(jnp.int32, (rows, 1), 0) + base
        place_row = lax.broadcasted_iota(jnp.int32, (1, rows), 1) + base
        end = jnp.int32(0)
        for r in range(requests):
            end = end + lengths_ref[0, r]
            request_col = request_col + (place_col >= end).astype(jnp.int32)
            request_row = request_row + (place_row >= end).astype(jnp.int32)
        shared = request_col == request_row
        inside = shared & (row_of >= col_of)
        after = shared & (row_of < col_of)
        strict = shared & (row_of > col_of)
        decay = decay_ref[:, here]
        pieces = jnp.concatenate([split_exact(decay), split_exact(beta_ref[:, here])], axis=0)
        inside_b = inside.astype(f32)
        masks = jnp.concatenate([inside_b, after.astype(f32), eye], axis=0)
        sums = product(masks, pieces, ((1,), (1,)))
        triple = lambda value, at: (
            value[:, at : at + heads]
            + value[:, at + heads : at + 2 * heads]
            + value[:, at + 2 * heads : at + 3 * heads]
        )
        running = triple(sums[:rows], 0)
        left = triple(sums[rows : 2 * rows], 0)
        strength = triple(sums[2 * rows :], 3 * heads)
        across = product(pieces[: 3 * heads], inside_b, ((1,), (1,)))
        running_t = across[:heads] + across[heads : 2 * heads] + across[2 * heads :]
        totals = [
            jnp.exp(jnp.sum(jnp.where(request_row == r, decay, 0.0), axis=1, keepdims=True))
            for r in range(requests)
        ]
        in_col = [request_col == r for r in range(requests)]
        in_row = [request_row == r for r in range(requests)]
        items = []
        for h in range(heads):
            lanes = slice(h * dim, (h + 1) * dim)
            key = key_ref[here, lanes].astype(f32)
            key = key * lax.rsqrt(jnp.sum(key * key, axis=-1, keepdims=True) + epsilon)
            query = query_ref[here, lanes].astype(f32)
            query = query * (
                lax.rsqrt(jnp.sum(query * query, axis=-1, keepdims=True) + epsilon)
                * dim ** (-0.5)
            )
            beta = strength[:, h : h + 1]
            gaps = running[:, h : h + 1] - running_t[h : h + 1, :]
            decays = jnp.where(inside, jnp.exp(jnp.minimum(gaps, 0.0)), 0.0)
            key_b = key.astype(bf16)
            both = product(
                jnp.concatenate([key_b, query.astype(bf16)], axis=0), key_b, ((1,), (1,))
            )
            growth = jnp.exp(running[:, h : h + 1])
            terms.append(jnp.where(strict, decays * both[:rows] * beta, 0.0).astype(bf16))
            targets = jnp.concatenate(
                [
                    (key * (beta * growth)).astype(bf16),
                    (value_ref[here, lanes].astype(f32) * beta).astype(bf16),
                ],
                axis=1,
            )
            items.append(
                (
                    targets,
                    (query * growth).astype(bf16),
                    (both[rows:] * decays).astype(bf16),
                    (key * jnp.exp(left[:, h : h + 1])).T.astype(bf16),
                )
            )
        chunks.append((here, items, totals, in_col, in_row))

    inverses = [eye - jnp.where(first, term.astype(f32), 0.0) for term in terms]
    count = len(terms)
    for mask in levels:
        narrow = [inverse.astype(bf16) for inverse in inverses]
        inner = [
            product(jnp.where(mask, terms[n], 0), narrow[n]).astype(bf16) for n in range(count)
        ]
        inverses = [inverses[n] - product(narrow[n], inner[n]) for n in range(count)]
    solutions = [
        product(inverses[n], chunks[n // heads][1][n % heads][0]) for n in range(count)
    ]

    for part, (here, items, totals, in_col, in_row) in enumerate(chunks):
        normed = []
        for h in range(heads):
            lanes = slice(h * dim, (h + 1) * dim)
            targets, query_g, dots, key_t = items[h]
            solved = solutions[part * heads + h]
            probe = jnp.concatenate([solved[:, :dim].astype(bf16), query_g], axis=0)
            wide = jnp.concatenate(
                [
                    jnp.where(jnp.concatenate([in_col[r], in_col[r]], axis=0), probe, 0)
                    for r in range(requests)
                ],
                axis=1,
            )
            seen = product(wide, states_ref[:, h].reshape(requests * dim, dim))
            update = (solved[:, dim:] - seen[:rows]).astype(bf16)
            mixed = seen[rows:] + product(dots, update)
            for r in range(requests):
                fresh = product(jnp.where(in_row[r], key_t, 0), update)
                states_ref[r, h] = totals[r][h : h + 1, :] * states_ref[r, h] + fresh
            scale = lax.rsqrt(jnp.mean(mixed * mixed, axis=-1, keepdims=True) + epsilon)
            gate = gate_ref[here, lanes].astype(f32)
            normed.append(
                (mixed * scale * gain_ref[...] * (gate * jax.nn.sigmoid(gate))).astype(bf16)
            )
        share = product(jnp.concatenate(normed, axis=1), proj_ref[...]).astype(bf16)
        for block in range(rows // owned):
            slot = part_slot("expert", (step * parts + part) * (rows // owned) + block)
            for place, share_ref in enumerate(share_refs):

                @pl.when(slot == place)
                def _(block=block, share=share, share_ref=share_ref):
                    share_ref[...] = share[block * owned : (block + 1) * owned]


def mix(queries, keys_in, values_in, gate_in, beta, decay, lengths, cache, norm_gain, out_proj, owned):
    tok_count, heads = beta.shape
    requests = lengths.shape[1]
    dim = norm_gain.shape[0]
    rows = min(chunk_rows, tok_count)
    taken = rows * (chunks_per_step if tok_count % (rows * chunks_per_step) == 0 else 1)
    width = out_proj.shape[1]
    block = lambda cols: pl.BlockSpec((taken, cols), lambda c: (c, 0))
    whole = lambda shape: pl.BlockSpec(shape, lambda c: (0,) * len(shape))
    return pl.pallas_call(
        functools.partial(mix_kernel, heads, requests, owned, rows),
        grid=(tok_count // taken,),
        in_specs=[
            block(heads * dim),
            block(heads * dim),
            block(heads * dim),
            block(heads * dim),
            pl.BlockSpec((heads, taken), lambda c: (0, c)),
            pl.BlockSpec((heads, taken), lambda c: (0, c)),
            pl.BlockSpec(memory_space=pltpu.SMEM),
            whole(cache.shape),
            whole((1, dim)),
            whole(out_proj.shape),
        ],
        out_specs=[whole(cache.shape)] + [whole((owned, width))] * (tok_count // owned),
        out_shape=[
            jax.ShapeDtypeStruct(cache.shape, jnp.float32),
        ]
        + [jax.ShapeDtypeStruct((owned, width), jnp.bfloat16)] * (tok_count // owned),
        compiler_params=pltpu.CompilerParams(
            dimension_semantics=("arbitrary",), vmem_limit_bytes=56 << 20
        ),
        cost_estimate=pl.CostEstimate(
            flops=40 * tok_count * heads * dim * dim * requests,
            bytes_accessed=12 * cache.size,
            transcendentals=0,
        ),
        name="mix",
    )(
        queries,
        keys_in,
        values_in,
        gate_in,
        beta.T,
        decay.T,
        lengths,
        cache,
        norm_gain[None],
        out_proj,
    )


def factors(size):
    low = 2 if size % 2 == 0 else 1
    return size // low, low


def partner(size, step, place):
    return place ^ step if size & (size - 1) == 0 else (place + step) % size


def source(size, step, place):
    return place ^ step if size & (size - 1) == 0 else (place - step) % size


def high_pairs(high, low, step):
    return [
        (h * low + m, partner(high, step, h) * low + m) for h in range(high) for m in range(low)
    ]


def low_pairs(high, low):
    return [(h * low + m, h * low + (m ^ 1)) for h in range(high) for m in range(low)]


def reverse(pairs):
    return [(target, origin) for origin, target in pairs]


def gather_parts(block, axis):
    high, low = factors(lax.axis_size(axis))
    parts = [[block]]
    for step in range(1, high):
        if high & (high - 1) == 0 and step & (step - 1):
            sent, hop = parts[step & (step - 1)][0], step & -step
        else:
            sent, hop = block, step
        parts.append([lax.ppermute(sent, axis, high_pairs(high, low, hop))])
    if low == 2:
        for row in parts:
            row.append(lax.ppermute(row[0], axis, low_pairs(high, low)))
    return parts


def scatter_parts(parts, axis, order):
    high, low = factors(lax.axis_size(axis))
    near = {}
    if low == 2:
        for step in order:
            near[step] = lax.ppermute(parts[step][1], axis, low_pairs(high, low))
    addends, before = [], None
    for step in order:
        pair = [parts[step][0]]
        if low == 2:
            other = near[step]
            if before is not None:
                other, before = lax.optimization_barrier((other, before))
            pair.append(other)
        if step == 0:
            addends += pair
            continue
        before = sum_parts(pair).astype(jnp.bfloat16)
        addends.append(lax.ppermute(before, axis, reverse(high_pairs(high, low, step))))
    return addends


def sum_parts(parts):
    total = parts[0].astype(jnp.float32)
    for part in parts[1:]:
        total = total + part.astype(jnp.float32)
    return total


def part_slot(axis, owner):
    high, low = factors(lax.axis_size(axis))
    place = lax.axis_index(axis)
    h, m = place // low, place % low
    other, n = owner // low, owner % low
    step = other ^ h if high & (high - 1) == 0 else (h - other + high) % high
    return step * low + (m ^ n)


def part_sources(axis):
    high, low = factors(lax.axis_size(axis))
    place = lax.axis_index(axis)
    h, m = place // low, place % low
    return [[source(high, step, h) * low + (m ^ j) for j in range(low)] for step in range(high)]


def on_device(
    queries,
    keys_in,
    values_in,
    gate_in,
    beta,
    decay,
    lengths,
    cache,
    norm_gain,
    out_proj,
    residual,
    post_gain,
    expert_ids,
    route_weights,
    gate_up,
    down_proj,
):
    tok_local = residual.shape[0]
    experts_all = lax.axis_size("expert") * lax.axis_size("dp")
    gate_up_parts = sum(gather_parts(gate_up[0], "dp"), [])
    down_parts = sum(gather_parts(down_proj[0], "dp"), [])
    expert_of = sum(part_sources("dp"), [])
    expert_of = [lax.axis_index("expert") * lax.axis_size("dp") + place for place in expert_of]
    new_states, *share = mix(
        queries,
        keys_in,
        values_in,
        gate_in,
        beta,
        decay,
        lengths,
        cache,
        norm_gain,
        out_proj,
        tok_local,
    )
    high, low = factors(lax.axis_size("expert"))
    shares = scatter_parts(
        [share[step * low : (step + 1) * low] for step in range(high)],
        "expert",
        range(high - 1, -1, -1),
    )
    expert_range = jnp.arange(experts_all, dtype=jnp.int32)
    mixing = jnp.sum(
        jnp.where(expert_ids[:, :, None] == expert_range, route_weights[:, :, None], 0.0), axis=1
    )
    coarse = mixing.astype(jnp.bfloat16)
    fine = (mixing - coarse.astype(jnp.float32)).astype(jnp.bfloat16)
    pad = jnp.zeros((tok_local, -2 * experts_all % 128), jnp.bfloat16)
    attn_out, block = close(
        shares, residual, post_gain, jnp.concatenate([coarse, fine, pad], axis=1)
    )
    gathered = gather_parts(block, "expert")
    places = jnp.stack(expert_of).astype(jnp.int32)
    half = high // 2
    middle = half + (high - half) // 2
    groups = [range(half, middle), range(middle, high), range(half)]
    results = {}
    for group in groups:
        blocks = [(step, j) for step in group for j in range(low)]
        if blocks:
            outs = experts(
                places,
                [gathered[step][j] for step, j in blocks],
                gate_up_parts,
                down_parts,
                experts_all,
            )
            results.update(zip(blocks, outs))
    moe_out = sum_parts(scatter_parts(
        [[results[step, j] for j in range(low)] for step in range(high)],
        "expert",
        [*groups[0], *groups[1], *reversed(groups[2])],
    )).astype(jnp.bfloat16)
    return (moe_out, attn_out, new_states)


def close_kernel(count, *refs):
    gain_ref, mixing_ref, attn_ref, block_ref, buffer, sems = refs[count:]
    width = attn_ref.shape[1]
    loads = [pltpu.make_async_copy(refs[n], buffer.at[n], sems.at[n]) for n in range(count)]
    for load in loads:
        load.start()
    for load in loads:
        load.wait()
    attn_ref[...] = sum_parts([buffer[n] for n in range(count)]).astype(jnp.bfloat16)
    stream = attn_ref[...].astype(jnp.float32)
    scale = lax.rsqrt(jnp.mean(stream * stream, axis=-1, keepdims=True) + epsilon)
    block_ref[:, :width] = (stream * scale * gain_ref[...]).astype(jnp.bfloat16)
    block_ref[:, width:] = mixing_ref[...]


def close(shares, residual, post_gain, mixing):
    rows, width = residual.shape
    parts = [residual, *shares]
    wide = width + mixing.shape[1]
    vmem = pl.BlockSpec(memory_space=pltpu.VMEM)
    return pl.pallas_call(
        functools.partial(close_kernel, len(parts)),
        in_specs=[pl.BlockSpec(memory_space=pl.ANY)] * len(parts) + [vmem] * 2,
        out_specs=[vmem] * 2,
        out_shape=[
            jax.ShapeDtypeStruct((rows, width), jnp.bfloat16),
            jax.ShapeDtypeStruct((rows, wide), jnp.bfloat16),
        ],
        scratch_shapes=[
            pltpu.VMEM((len(parts), rows, width), jnp.bfloat16),
            pltpu.SemaphoreType.DMA((len(parts),)),
        ],
        compiler_params=pltpu.CompilerParams(vmem_limit_bytes=16 << 20),
        name="close",
    )(*parts, post_gain[None], mixing)


def experts_kernel(blocks, slots, experts_all, places_ref, *refs):
    row_refs = refs[:blocks]
    gate_up_refs = refs[blocks : blocks + slots]
    down_refs = refs[blocks + slots : blocks + 2 * slots]
    out_refs = refs[blocks + 2 * slots : 2 * blocks + 2 * slots]
    hidden_buf = refs[2 * blocks + 2 * slots]
    width, hidden_width = gate_up_refs[0].shape[0], down_refs[0].shape[0]
    rows = jnp.concatenate([ref[:, :width] for ref in row_refs], axis=0)
    mixing = jnp.concatenate([ref[:, width:] for ref in row_refs], axis=0).astype(jnp.float32)
    lane = lax.broadcasted_iota(jnp.int32, mixing.shape, 1)
    for i in range(slots):
        place = places_ref[i]
        named = (lane == place) | (lane == place + experts_all)
        weight = jnp.sum(jnp.where(named, mixing, 0.0), axis=1, keepdims=True)
        both = product(rows, gate_up_refs[i][...])
        gate = both[:, :hidden_width]
        hidden = gate * jax.nn.sigmoid(gate) * both[:, hidden_width:] * weight
        hidden_buf[:, i * hidden_width : (i + 1) * hidden_width] = hidden.astype(jnp.bfloat16)
    size = row_refs[0].shape[0]
    tile = min(512, width)
    for start in range(0, width, tile):
        down = jnp.concatenate([ref[:, start : start + tile] for ref in down_refs], axis=0)
        result = product(hidden_buf[...], down).astype(jnp.bfloat16)
        for n in range(blocks):
            out_refs[n][:, start : start + tile] = result[n * size : (n + 1) * size]


def experts(places, row_blocks, gate_up_parts, down_parts, experts_all):
    blocks, slots = len(row_blocks), len(gate_up_parts)
    size = row_blocks[0].shape[0]
    width, hidden_twice = gate_up_parts[0].shape
    hidden_width = down_parts[0].shape[0]
    vmem = pl.BlockSpec(memory_space=pltpu.VMEM)
    return pl.pallas_call(
        functools.partial(experts_kernel, blocks, slots, experts_all),
        in_specs=[pl.BlockSpec(memory_space=pltpu.SMEM)]
        + [vmem] * (blocks + 2 * slots),
        out_specs=[vmem] * blocks,
        out_shape=[jax.ShapeDtypeStruct((size, width), jnp.bfloat16)] * blocks,
        scratch_shapes=[
            pltpu.VMEM((blocks * size, slots * hidden_width), jnp.bfloat16),
        ],
        cost_estimate=pl.CostEstimate(
            flops=2 * blocks * size * slots * width * (hidden_twice + hidden_width),
            bytes_accessed=4 * blocks * size * width,
            transcendentals=0,
        ),
        compiler_params=pltpu.CompilerParams(
            vmem_limit_bytes=(12 << 20)
            + 2 * slots * width * (hidden_twice + hidden_width)
        ),
        name="experts",
    )(places, *row_blocks, *gate_up_parts, *down_parts)


def solution(mesh):
    return jax.shard_map(
        on_device,
        mesh=mesh,
        in_specs=(
            P(("groups", "dp"), "expert"),
            P(("groups", "dp"), "expert"),
            P(("groups", "dp"), "expert"),
            P(("groups", "dp"), "expert"),
            P(("groups", "dp"), "expert"),
            P(("groups", "dp"), "expert"),
            P(("groups", "dp"), None),
            P(("groups", "dp"), "expert", None, None),
            P(),
            P("expert", None),
            P(("groups", "dp", "expert"), None),
            P(),
            P(("groups", "dp", "expert"), None),
            P(("groups", "dp", "expert"), None),
            P(("expert", "dp"), None, None),
            P(("expert", "dp"), None, None),
        ),
        out_specs=(
            P(("groups", "dp", "expert"), None),
            P(("groups", "dp", "expert"), None),
            P(("groups", "dp"), "expert", None, None),
        ),
        check_vma=False,
    )
```

```python
import functools

import jax
import jax.numpy as jnp
from jax import lax
from jax.experimental import pallas as pl
from jax.experimental.pallas import tpu as pltpu
from jax.sharding import PartitionSpec as P


epsilon = 1e-06
chunk_rows = 128
chunks_per_step = 2


def product(left, right, contract=((1,), (0,))):
    left, right = left.astype(jnp.bfloat16), right.astype(jnp.bfloat16)
    return lax.dot_general(left, right, (contract, ((), ())), preferred_element_type=jnp.float32)


def split_exact(value):
    parts = []
    for _ in range(3):
        part = value.astype(jnp.bfloat16)
        parts.append(part)
        value = value - part.astype(jnp.float32)
    return jnp.concatenate(parts, axis=0)


def mix_kernel(
    heads,
    requests,
    owned,
    rows,
    query_ref,
    key_ref,
    value_ref,
    gate_ref,
    beta_ref,
    decay_ref,
    lengths_ref,
    cache_ref,
    gain_ref,
    proj_ref,
    states_ref,
    *share_refs,
):
    step = pl.program_id(0)
    parts = query_ref.shape[0] // rows
    dim = gain_ref.shape[1]
    f32, bf16 = jnp.float32, jnp.bfloat16

    @pl.when(step == 0)
    def _():
        states_ref[...] = cache_ref[...]

    row_of = lax.broadcasted_iota(jnp.int32, (rows, rows), 0)
    col_of = lax.broadcasted_iota(jnp.int32, (rows, rows), 1)
    eye = (row_of == col_of).astype(f32)
    levels = []
    span = 2
    while span < rows:
        levels.append(
            (row_of // (2 * span) == col_of // (2 * span))
            & ((row_of // span) % 2 == 1)
            & ((col_of // span) % 2 == 0)
        )
        span *= 2
    first = (row_of // 2 == col_of // 2) & (row_of != col_of)

    chunks, terms = [], []
    for part in range(parts):
        here = slice(part * rows, (part + 1) * rows)
        request_col = jnp.zeros((rows, 1), jnp.int32)
        request_row = jnp.zeros((1, rows), jnp.int32)
        base = (step * parts + part) * rows
        place_col = lax.broadcasted_iota(jnp.int32, (rows, 1), 0) + base
        place_row = lax.broadcasted_iota(jnp.int32, (1, rows), 1) + base
        end = jnp.int32(0)
        for r in range(requests):
            end = end + lengths_ref[0, r]
            request_col = request_col + (place_col >= end).astype(jnp.int32)
            request_row = request_row + (place_row >= end).astype(jnp.int32)
        shared = request_col == request_row
        inside = shared & (row_of >= col_of)
        after = shared & (row_of < col_of)
        strict = shared & (row_of > col_of)
        decay = decay_ref[:, here]
        pieces = jnp.concatenate([split_exact(decay), split_exact(beta_ref[:, here])], axis=0)
        inside_b = inside.astype(f32)
        masks = jnp.concatenate([inside_b, after.astype(f32), eye], axis=0)
        sums = product(masks, pieces, ((1,), (1,)))
        triple = lambda value, at: (
            value[:, at : at + heads]
            + value[:, at + heads : at + 2 * heads]
            + value[:, at + 2 * heads : at + 3 * heads]
        )
        running = triple(sums[:rows], 0)
        left = triple(sums[rows : 2 * rows], 0)
        strength = triple(sums[2 * rows :], 3 * heads)
        across = product(pieces[: 3 * heads], inside_b, ((1,), (1,)))
        running_t = across[:heads] + across[heads : 2 * heads] + across[2 * heads :]
        totals = [
            jnp.exp(jnp.sum(jnp.where(request_row == r, decay, 0.0), axis=1, keepdims=True))
            for r in range(requests)
        ]
        in_col = [request_col == r for r in range(requests)]
        in_row = [request_row == r for r in range(requests)]
        items = []
        for h in range(heads):
            lanes = slice(h * dim, (h + 1) * dim)
            key = key_ref[here, lanes].astype(f32)
            key = key * lax.rsqrt(jnp.sum(key * key, axis=-1, keepdims=True) + epsilon)
            query = query_ref[here, lanes].astype(f32)
            query = query * (
                lax.rsqrt(jnp.sum(query * query, axis=-1, keepdims=True) + epsilon)
                * dim ** (-0.5)
            )
            beta = strength[:, h : h + 1]
            gaps = running[:, h : h + 1] - running_t[h : h + 1, :]
            decays = jnp.where(inside, jnp.exp(jnp.minimum(gaps, 0.0)), 0.0)
            key_b = key.astype(bf16)
            both = product(
                jnp.concatenate([key_b, query.astype(bf16)], axis=0), key_b, ((1,), (1,))
            )
            growth = jnp.exp(running[:, h : h + 1])
            terms.append(jnp.where(strict, decays * both[:rows] * beta, 0.0).astype(bf16))
            targets = jnp.concatenate(
                [
                    (key * (beta * growth)).astype(bf16),
                    (value_ref[here, lanes].astype(f32) * beta).astype(bf16),
                ],
                axis=1,
            )
            items.append(
                (
                    targets,
                    (query * growth).astype(bf16),
                    (both[rows:] * decays).astype(bf16),
                    (key * jnp.exp(left[:, h : h + 1])).T.astype(bf16),
                )
            )
        chunks.append((here, items, totals, in_col, in_row))

    inverses = [eye - jnp.where(first, term.astype(f32), 0.0) for term in terms]
    count = len(terms)
    for mask in levels:
        narrow = [inverse.astype(bf16) for inverse in inverses]
        inner = [
            product(jnp.where(mask, terms[n], 0), narrow[n]).astype(bf16) for n in range(count)
        ]
        inverses = [inverses[n] - product(narrow[n], inner[n]) for n in range(count)]
    solutions = [
        product(inverses[n], chunks[n // heads][1][n % heads][0]) for n in range(count)
    ]

    for part, (here, items, totals, in_col, in_row) in enumerate(chunks):
        normed = []
        for h in range(heads):
            lanes = slice(h * dim, (h + 1) * dim)
            targets, query_g, dots, key_t = items[h]
            solved = solutions[part * heads + h]
            probe = jnp.concatenate([solved[:, :dim].astype(bf16), query_g], axis=0)
            wide = jnp.concatenate(
                [
                    jnp.where(jnp.concatenate([in_col[r], in_col[r]], axis=0), probe, 0)
                    for r in range(requests)
                ],
                axis=1,
            )
            seen = product(wide, states_ref[:, h].reshape(requests * dim, dim))
            update = (solved[:, dim:] - seen[:rows]).astype(bf16)
            mixed = seen[rows:] + product(dots, update)
            for r in range(requests):
                fresh = product(jnp.where(in_row[r], key_t, 0), update)
                states_ref[r, h] = totals[r][h : h + 1, :] * states_ref[r, h] + fresh
            scale = lax.rsqrt(jnp.mean(mixed * mixed, axis=-1, keepdims=True) + epsilon)
            gate = gate_ref[here, lanes].astype(f32)
            normed.append(
                (mixed * scale * gain_ref[...] * (gate * jax.nn.sigmoid(gate))).astype(bf16)
            )
        share = product(jnp.concatenate(normed, axis=1), proj_ref[...]).astype(bf16)
        for block in range(rows // owned):
            slot = part_slot("expert", (step * parts + part) * (rows // owned) + block)
            for place, share_ref in enumerate(share_refs):

                @pl.when(slot == place)
                def _(block=block, share=share, share_ref=share_ref):
                    share_ref[...] = share[block * owned : (block + 1) * owned]


def mix(queries, keys_in, values_in, gate_in, beta, decay, lengths, cache, norm_gain, out_proj, owned):
    tok_count, heads = beta.shape
    requests = lengths.shape[1]
    dim = norm_gain.shape[0]
    rows = min(chunk_rows, tok_count)
    taken = rows * (chunks_per_step if tok_count % (rows * chunks_per_step) == 0 else 1)
    width = out_proj.shape[1]
    block = lambda cols: pl.BlockSpec((taken, cols), lambda c: (c, 0))
    whole = lambda shape: pl.BlockSpec(shape, lambda c: (0,) * len(shape))
    return pl.pallas_call(
        functools.partial(mix_kernel, heads, requests, owned, rows),
        grid=(tok_count // taken,),
        in_specs=[
            block(heads * dim),
            block(heads * dim),
            block(heads * dim),
            block(heads * dim),
            pl.BlockSpec((heads, taken), lambda c: (0, c)),
            pl.BlockSpec((heads, taken), lambda c: (0, c)),
            pl.BlockSpec(memory_space=pltpu.SMEM),
            whole(cache.shape),
            whole((1, dim)),
            whole(out_proj.shape),
        ],
        out_specs=[whole(cache.shape)] + [whole((owned, width))] * (tok_count // owned),
        out_shape=[
            jax.ShapeDtypeStruct(cache.shape, jnp.float32),
        ]
        + [jax.ShapeDtypeStruct((owned, width), jnp.bfloat16)] * (tok_count // owned),
        compiler_params=pltpu.CompilerParams(
            dimension_semantics=("arbitrary",), vmem_limit_bytes=56 << 20
        ),
        cost_estimate=pl.CostEstimate(
            flops=40 * tok_count * heads * dim * dim * requests,
            bytes_accessed=12 * cache.size,
            transcendentals=0,
        ),
        name="mix",
    )(
        queries,
        keys_in,
        values_in,
        gate_in,
        beta.T,
        decay.T,
        lengths,
        cache,
        norm_gain[None],
        out_proj,
    )


def factors(size):
    low = 2 if size % 2 == 0 else 1
    return size // low, low


def partner(size, step, place):
    return place ^ step if size & (size - 1) == 0 else (place + step) % size


def source(size, step, place):
    return place ^ step if size & (size - 1) == 0 else (place - step) % size


def high_pairs(high, low, step):
    return [
        (h * low + m, partner(high, step, h) * low + m) for h in range(high) for m in range(low)
    ]


def low_pairs(high, low):
    return [(h * low + m, h * low + (m ^ 1)) for h in range(high) for m in range(low)]


def reverse(pairs):
    return [(target, origin) for origin, target in pairs]


def gather_parts(block, axis):
    high, low = factors(lax.axis_size(axis))
    parts = [[block]]
    for step in range(1, high):
        if high & (high - 1) == 0 and step & (step - 1):
            sent, hop = parts[step & (step - 1)][0], step & -step
        else:
            sent, hop = block, step
        parts.append([lax.ppermute(sent, axis, high_pairs(high, low, hop))])
    if low == 2:
        for row in parts:
            row.append(lax.ppermute(row[0], axis, low_pairs(high, low)))
    return parts


def scatter_parts(parts, axis, order):
    high, low = factors(lax.axis_size(axis))
    near = {}
    if low == 2:
        for step in order:
            near[step] = lax.ppermute(parts[step][1], axis, low_pairs(high, low))
    own, rest, before = [], [], None
    for step in order:
        pair = [parts[step][0]]
        if low == 2:
            other = near[step]
            if before is not None:
                other, before = lax.optimization_barrier((other, before))
            pair.append(other)
        if step == 0:
            own = pair
            continue
        before = sum_parts(pair).astype(jnp.bfloat16)
        rest.append(lax.ppermute(before, axis, reverse(high_pairs(high, low, step))))
    return own, rest


def sum_parts(parts):
    total = parts[0].astype(jnp.float32)
    for part in parts[1:]:
        total = total + part.astype(jnp.float32)
    return total


def part_slot(axis, owner):
    high, low = factors(lax.axis_size(axis))
    place = lax.axis_index(axis)
    h, m = place // low, place % low
    other, n = owner // low, owner % low
    step = other ^ h if high & (high - 1) == 0 else (h - other + high) % high
    return step * low + (m ^ n)


def part_sources(axis):
    high, low = factors(lax.axis_size(axis))
    place = lax.axis_index(axis)
    h, m = place // low, place % low
    return [[source(high, step, h) * low + (m ^ j) for j in range(low)] for step in range(high)]


def on_device(
    queries,
    keys_in,
    values_in,
    gate_in,
    beta,
    decay,
    lengths,
    cache,
    norm_gain,
    out_proj,
    residual,
    post_gain,
    expert_ids,
    route_weights,
    gate_up,
    down_proj,
):
    tok_local = residual.shape[0]
    experts_all = lax.axis_size("expert") * lax.axis_size("dp")
    gate_up_parts = sum(gather_parts(gate_up[0], "dp"), [])
    down_parts = sum(gather_parts(down_proj[0], "dp"), [])
    expert_of = sum(part_sources("dp"), [])
    expert_of = [lax.axis_index("expert") * lax.axis_size("dp") + place for place in expert_of]
    new_states, *share = mix(
        queries,
        keys_in,
        values_in,
        gate_in,
        beta,
        decay,
        lengths,
        cache,
        norm_gain,
        out_proj,
        tok_local,
    )
    high, low = factors(lax.axis_size("expert"))
    own, rest = scatter_parts(
        [share[step * low : (step + 1) * low] for step in range(high)],
        "expert",
        range(high - 1, -1, -1),
    )
    expert_range = jnp.arange(experts_all, dtype=jnp.int32)
    mixing = jnp.sum(
        jnp.where(expert_ids[:, :, None] == expert_range, route_weights[:, :, None], 0.0), axis=1
    )
    coarse = mixing.astype(jnp.bfloat16)
    fine = (mixing - coarse.astype(jnp.float32)).astype(jnp.bfloat16)
    pad = jnp.zeros((tok_local, -2 * experts_all % 128), jnp.bfloat16)
    attn_out, block = close(
        sum_parts([residual, *own]),
        rest,
        post_gain,
        jnp.concatenate([coarse, fine, pad], axis=1),
    )
    gathered = gather_parts(block, "expert")
    places = jnp.stack(expert_of).astype(jnp.int32)
    half = high // 2
    middle = half + (high - half) // 2
    groups = [range(half, middle), range(middle, high), range(half)]
    results = {}
    for group in groups:
        blocks = [(step, j) for step in group for j in range(low)]
        if blocks:
            outs = experts(
                places,
                [gathered[step][j] for step, j in blocks],
                gate_up_parts,
                down_parts,
                experts_all,
            )
            results.update(zip(blocks, outs))
    own, rest = scatter_parts(
        [[results[step, j] for j in range(low)] for step in range(high)],
        "expert",
        [*groups[0], *groups[1], *reversed(groups[2])],
    )
    moe_out = sum_parts([*own, *rest]).astype(jnp.bfloat16)
    return (moe_out, attn_out, new_states)


def close_kernel(count, base_ref, *refs):
    gain_ref, mixing_ref, attn_ref, block_ref = refs[count:]
    width = attn_ref.shape[1]
    total = sum_parts([base_ref[...]] + [ref[...] for ref in refs[:count]])
    attn_ref[...] = total.astype(jnp.bfloat16)
    stream = attn_ref[...].astype(jnp.float32)
    scale = lax.rsqrt(jnp.mean(stream * stream, axis=-1, keepdims=True) + epsilon)
    block_ref[:, :width] = (stream * scale * gain_ref[...]).astype(jnp.bfloat16)
    block_ref[:, width:] = mixing_ref[...]


def close(base, rest, post_gain, mixing):
    rows, width = base.shape
    vmem = pl.BlockSpec(memory_space=pltpu.VMEM)
    return pl.pallas_call(
        functools.partial(close_kernel, len(rest)),
        in_specs=[vmem] * (len(rest) + 3),
        out_specs=[vmem] * 2,
        out_shape=[
            jax.ShapeDtypeStruct((rows, width), jnp.bfloat16),
            jax.ShapeDtypeStruct((rows, width + mixing.shape[1]), jnp.bfloat16),
        ],
        compiler_params=pltpu.CompilerParams(vmem_limit_bytes=8 << 20),
        name="close",
    )(base, *rest, post_gain[None], mixing)


def experts_kernel(blocks, slots, experts_all, places_ref, *refs):
    row_refs = refs[:blocks]
    gate_up_refs = refs[blocks : blocks + slots]
    down_refs = refs[blocks + slots : blocks + 2 * slots]
    out_refs = refs[blocks + 2 * slots : 2 * blocks + 2 * slots]
    hidden_buf = refs[2 * blocks + 2 * slots]
    width, hidden_width = gate_up_refs[0].shape[0], down_refs[0].shape[0]
    rows = jnp.concatenate([ref[:, :width] for ref in row_refs], axis=0)
    mixing = jnp.concatenate([ref[:, width:] for ref in row_refs], axis=0).astype(jnp.float32)
    lane = lax.broadcasted_iota(jnp.int32, mixing.shape, 1)
    for i in range(slots):
        place = places_ref[i]
        named = (lane == place) | (lane == place + experts_all)
        weight = jnp.sum(jnp.where(named, mixing, 0.0), axis=1, keepdims=True)
        both = product(rows, gate_up_refs[i][...])
        gate = both[:, :hidden_width]
        hidden = gate * jax.nn.sigmoid(gate) * both[:, hidden_width:] * weight
        hidden_buf[:, i * hidden_width : (i + 1) * hidden_width] = hidden.astype(jnp.bfloat16)
    size = row_refs[0].shape[0]
    tile = min(512, width)
    for start in range(0, width, tile):
        down = jnp.concatenate([ref[:, start : start + tile] for ref in down_refs], axis=0)
        result = product(hidden_buf[...], down).astype(jnp.bfloat16)
        for n in range(blocks):
            out_refs[n][:, start : start + tile] = result[n * size : (n + 1) * size]


def experts(places, row_blocks, gate_up_parts, down_parts, experts_all):
    blocks, slots = len(row_blocks), len(gate_up_parts)
    size = row_blocks[0].shape[0]
    width, hidden_twice = gate_up_parts[0].shape
    hidden_width = down_parts[0].shape[0]
    vmem = pl.BlockSpec(memory_space=pltpu.VMEM)
    return pl.pallas_call(
        functools.partial(experts_kernel, blocks, slots, experts_all),
        in_specs=[pl.BlockSpec(memory_space=pltpu.SMEM)]
        + [vmem] * (blocks + 2 * slots),
        out_specs=[vmem] * blocks,
        out_shape=[jax.ShapeDtypeStruct((size, width), jnp.bfloat16)] * blocks,
        scratch_shapes=[
            pltpu.VMEM((blocks * size, slots * hidden_width), jnp.bfloat16),
        ],
        cost_estimate=pl.CostEstimate(
            flops=2 * blocks * size * slots * width * (hidden_twice + hidden_width),
            bytes_accessed=4 * blocks * size * width,
            transcendentals=0,
        ),
        compiler_params=pltpu.CompilerParams(
            vmem_limit_bytes=(12 << 20)
            + 2 * slots * width * (hidden_twice + hidden_width)
        ),
        name="experts",
    )(places, *row_blocks, *gate_up_parts, *down_parts)


def solution(mesh):
    return jax.shard_map(
        on_device,
        mesh=mesh,
        in_specs=(
            P(("groups", "dp"), "expert"),
            P(("groups", "dp"), "expert"),
            P(("groups", "dp"), "expert"),
            P(("groups", "dp"), "expert"),
            P(("groups", "dp"), "expert"),
            P(("groups", "dp"), "expert"),
            P(("groups", "dp"), None),
            P(("groups", "dp"), "expert", None, None),
            P(),
            P("expert", None),
            P(("groups", "dp", "expert"), None),
            P(),
            P(("groups", "dp", "expert"), None),
            P(("groups", "dp", "expert"), None),
            P(("expert", "dp"), None, None),
            P(("expert", "dp"), None, None),
        ),
        out_specs=(
            P(("groups", "dp", "expert"), None),
            P(("groups", "dp", "expert"), None),
            P(("groups", "dp"), "expert", None, None),
        ),
        check_vma=False,
    )
```

```python
import functools

import jax
import jax.numpy as jnp
from jax import lax
from jax.experimental import pallas as pl
from jax.experimental.pallas import tpu as pltpu
from jax.sharding import PartitionSpec as P


epsilon = 1e-06
chunk_rows = 128
chunks_per_step = 4


def product(left, right, contract=((1,), (0,))):
    left, right = left.astype(jnp.bfloat16), right.astype(jnp.bfloat16)
    return lax.dot_general(left, right, (contract, ((), ())), preferred_element_type=jnp.float32)


def split_exact(value):
    parts = []
    for _ in range(3):
        part = value.astype(jnp.bfloat16)
        parts.append(part)
        value = value - part.astype(jnp.float32)
    return jnp.concatenate(parts, axis=0)


def mix_kernel(
    heads,
    requests,
    owned,
    rows,
    query_ref,
    key_ref,
    value_ref,
    gate_ref,
    beta_ref,
    decay_ref,
    lengths_ref,
    cache_ref,
    gain_ref,
    proj_ref,
    states_ref,
    *share_refs,
):
    step = pl.program_id(0)
    parts = query_ref.shape[0] // rows
    dim = gain_ref.shape[1]
    f32, bf16 = jnp.float32, jnp.bfloat16

    @pl.when(step == 0)
    def _():
        states_ref[...] = cache_ref[...]

    row_of = lax.broadcasted_iota(jnp.int32, (rows, rows), 0)
    col_of = lax.broadcasted_iota(jnp.int32, (rows, rows), 1)
    eye = (row_of == col_of).astype(f32)
    levels = []
    span = 2
    while span < rows:
        levels.append(
            (row_of // (2 * span) == col_of // (2 * span))
            & ((row_of // span) % 2 == 1)
            & ((col_of // span) % 2 == 0)
        )
        span *= 2
    first = (row_of // 2 == col_of // 2) & (row_of != col_of)

    chunks, terms = [], []
    for part in range(parts):
        here = slice(part * rows, (part + 1) * rows)
        request_col = jnp.zeros((rows, 1), jnp.int32)
        request_row = jnp.zeros((1, rows), jnp.int32)
        base = (step * parts + part) * rows
        place_col = lax.broadcasted_iota(jnp.int32, (rows, 1), 0) + base
        place_row = lax.broadcasted_iota(jnp.int32, (1, rows), 1) + base
        end = jnp.int32(0)
        for r in range(requests):
            end = end + lengths_ref[0, r]
            request_col = request_col + (place_col >= end).astype(jnp.int32)
            request_row = request_row + (place_row >= end).astype(jnp.int32)
        shared = request_col == request_row
        inside = shared & (row_of >= col_of)
        after = shared & (row_of < col_of)
        strict = shared & (row_of > col_of)
        decay = decay_ref[:, here]
        pieces = jnp.concatenate([split_exact(decay), split_exact(beta_ref[:, here])], axis=0)
        inside_b = inside.astype(f32)
        masks = jnp.concatenate([inside_b, after.astype(f32), eye], axis=0)
        sums = product(masks, pieces, ((1,), (1,)))
        triple = lambda value, at: (
            value[:, at : at + heads]
            + value[:, at + heads : at + 2 * heads]
            + value[:, at + 2 * heads : at + 3 * heads]
        )
        running = triple(sums[:rows], 0)
        left = triple(sums[rows : 2 * rows], 0)
        strength = triple(sums[2 * rows :], 3 * heads)
        across = product(pieces[: 3 * heads], inside_b, ((1,), (1,)))
        running_t = across[:heads] + across[heads : 2 * heads] + across[2 * heads :]
        totals = [
            jnp.exp(jnp.sum(jnp.where(request_row == r, decay, 0.0), axis=1, keepdims=True))
            for r in range(requests)
        ]
        in_col = [request_col == r for r in range(requests)]
        in_row = [request_row == r for r in range(requests)]
        items = []
        for h in range(heads):
            lanes = slice(h * dim, (h + 1) * dim)
            key = key_ref[here, lanes].astype(f32)
            key = key * lax.rsqrt(jnp.sum(key * key, axis=-1, keepdims=True) + epsilon)
            query = query_ref[here, lanes].astype(f32)
            query = query * (
                lax.rsqrt(jnp.sum(query * query, axis=-1, keepdims=True) + epsilon)
                * dim ** (-0.5)
            )
            beta = strength[:, h : h + 1]
            gaps = running[:, h : h + 1] - running_t[h : h + 1, :]
            decays = jnp.where(inside, jnp.exp(jnp.minimum(gaps, 0.0)), 0.0)
            key_b = key.astype(bf16)
            both = product(
                jnp.concatenate([key_b, query.astype(bf16)], axis=0), key_b, ((1,), (1,))
            )
            growth = jnp.exp(running[:, h : h + 1])
            terms.append(jnp.where(strict, decays * both[:rows] * beta, 0.0).astype(bf16))
            targets = jnp.concatenate(
                [
                    (key * (beta * growth)).astype(bf16),
                    (value_ref[here, lanes].astype(f32) * beta).astype(bf16),
                ],
                axis=1,
            )
            items.append(
                (
                    targets,
                    (query * growth).astype(bf16),
                    (both[rows:] * decays).astype(bf16),
                    (key * jnp.exp(left[:, h : h + 1])).T.astype(bf16),
                )
            )
        chunks.append((here, items, totals, in_col, in_row))

    inverses = [eye - jnp.where(first, term.astype(f32), 0.0) for term in terms]
    count = len(terms)
    for mask in levels:
        narrow = [inverse.astype(bf16) for inverse in inverses]
        inner = [
            product(jnp.where(mask, terms[n], 0), narrow[n]).astype(bf16) for n in range(count)
        ]
        inverses = [inverses[n] - product(narrow[n], inner[n]) for n in range(count)]
    solutions = [
        product(inverses[n], chunks[n // heads][1][n % heads][0]) for n in range(count)
    ]

    for part, (here, items, totals, in_col, in_row) in enumerate(chunks):
        normed = []
        for h in range(heads):
            lanes = slice(h * dim, (h + 1) * dim)
            targets, query_g, dots, key_t = items[h]
            solved = solutions[part * heads + h]
            probe = jnp.concatenate([solved[:, :dim].astype(bf16), query_g], axis=0)
            wide = jnp.concatenate(
                [
                    jnp.where(jnp.concatenate([in_col[r], in_col[r]], axis=0), probe, 0)
                    for r in range(requests)
                ],
                axis=1,
            )
            seen = product(wide, states_ref[:, h].reshape(requests * dim, dim))
            update = (solved[:, dim:] - seen[:rows]).astype(bf16)
            mixed = seen[rows:] + product(dots, update)
            for r in range(requests):
                fresh = product(jnp.where(in_row[r], key_t, 0), update)
                states_ref[r, h] = totals[r][h : h + 1, :] * states_ref[r, h] + fresh
            scale = lax.rsqrt(jnp.mean(mixed * mixed, axis=-1, keepdims=True) + epsilon)
            gate = gate_ref[here, lanes].astype(f32)
            normed.append(
                (mixed * scale * gain_ref[...] * (gate * jax.nn.sigmoid(gate))).astype(bf16)
            )
        share = product(jnp.concatenate(normed, axis=1), proj_ref[...]).astype(bf16)
        for block in range(rows // owned):
            slot = part_slot("expert", (step * parts + part) * (rows // owned) + block)
            for place, share_ref in enumerate(share_refs):

                @pl.when(slot == place)
                def _(block=block, share=share, share_ref=share_ref):
                    share_ref[...] = share[block * owned : (block + 1) * owned]


def mix(queries, keys_in, values_in, gate_in, beta, decay, lengths, cache, norm_gain, out_proj, owned):
    tok_count, heads = beta.shape
    requests = lengths.shape[1]
    dim = norm_gain.shape[0]
    rows = min(chunk_rows, tok_count)
    taken = rows * (chunks_per_step if tok_count % (rows * chunks_per_step) == 0 else 1)
    width = out_proj.shape[1]
    block = lambda cols: pl.BlockSpec((taken, cols), lambda c: (c, 0))
    whole = lambda shape: pl.BlockSpec(shape, lambda c: (0,) * len(shape))
    return pl.pallas_call(
        functools.partial(mix_kernel, heads, requests, owned, rows),
        grid=(tok_count // taken,),
        in_specs=[
            block(heads * dim),
            block(heads * dim),
            block(heads * dim),
            block(heads * dim),
            pl.BlockSpec((heads, taken), lambda c: (0, c)),
            pl.BlockSpec((heads, taken), lambda c: (0, c)),
            pl.BlockSpec(memory_space=pltpu.SMEM),
            whole(cache.shape),
            whole((1, dim)),
            whole(out_proj.shape),
        ],
        out_specs=[whole(cache.shape)] + [whole((owned, width))] * (tok_count // owned),
        out_shape=[
            jax.ShapeDtypeStruct(cache.shape, jnp.float32),
        ]
        + [jax.ShapeDtypeStruct((owned, width), jnp.bfloat16)] * (tok_count // owned),
        compiler_params=pltpu.CompilerParams(
            dimension_semantics=("arbitrary",), vmem_limit_bytes=56 << 20
        ),
        cost_estimate=pl.CostEstimate(
            flops=40 * tok_count * heads * dim * dim * requests,
            bytes_accessed=12 * cache.size,
            transcendentals=0,
        ),
        name="mix",
    )(
        queries,
        keys_in,
        values_in,
        gate_in,
        beta.T,
        decay.T,
        lengths,
        cache,
        norm_gain[None],
        out_proj,
    )


def factors(size):
    low = 2 if size % 2 == 0 else 1
    return size // low, low


def partner(size, step, place):
    return place ^ step if size & (size - 1) == 0 else (place + step) % size


def source(size, step, place):
    return place ^ step if size & (size - 1) == 0 else (place - step) % size


def high_pairs(high, low, step):
    return [
        (h * low + m, partner(high, step, h) * low + m) for h in range(high) for m in range(low)
    ]


def low_pairs(high, low):
    return [(h * low + m, h * low + (m ^ 1)) for h in range(high) for m in range(low)]


def reverse(pairs):
    return [(target, origin) for origin, target in pairs]


def gather_parts(block, axis, around=False):
    high, low = factors(lax.axis_size(axis))
    parts = [[block]]
    for step in range(1, high):
        if high & (high - 1) == 0 and step & (step - 1):
            sent, hop = parts[step & (step - 1)][0], step & -step
        else:
            sent, hop = block, step
        parts.append([lax.ppermute(sent, axis, high_pairs(high, low, hop))])
    if low == 2:
        for step, row in enumerate(parts):
            if around and step == 1:
                row.append(lax.ppermute(parts[0][1], axis, high_pairs(high, low, step)))
            else:
                row.append(lax.ppermute(row[0], axis, low_pairs(high, low)))
    return parts


def scatter_parts(parts, axis, order):
    high, low = factors(lax.axis_size(axis))
    near = {}
    if low == 2:
        for step in order:
            near[step] = lax.ppermute(parts[step][1], axis, low_pairs(high, low))
    own, rest, before = [], [], None
    for step in order:
        pair = [parts[step][0]]
        if low == 2:
            other = near[step]
            if before is not None:
                other, before = lax.optimization_barrier((other, before))
            pair.append(other)
        if step == 0:
            own = pair
            continue
        before = sum_parts(pair).astype(jnp.bfloat16)
        rest.append(lax.ppermute(before, axis, reverse(high_pairs(high, low, step))))
    return own, rest


def sum_parts(parts):
    total = parts[0].astype(jnp.float32)
    for part in parts[1:]:
        total = total + part.astype(jnp.float32)
    return total


def part_slot(axis, owner):
    high, low = factors(lax.axis_size(axis))
    place = lax.axis_index(axis)
    h, m = place // low, place % low
    other, n = owner // low, owner % low
    step = other ^ h if high & (high - 1) == 0 else (h - other + high) % high
    return step * low + (m ^ n)


def part_sources(axis):
    high, low = factors(lax.axis_size(axis))
    place = lax.axis_index(axis)
    h, m = place // low, place % low
    return [[source(high, step, h) * low + (m ^ j) for j in range(low)] for step in range(high)]


def on_device(
    queries,
    keys_in,
    values_in,
    gate_in,
    beta,
    decay,
    lengths,
    cache,
    norm_gain,
    out_proj,
    residual,
    post_gain,
    expert_ids,
    route_weights,
    gate_up,
    down_proj,
):
    tok_local = residual.shape[0]
    experts_all = lax.axis_size("expert") * lax.axis_size("dp")
    gate_up_parts = sum(gather_parts(gate_up[0], "dp"), [])
    down_parts = sum(gather_parts(down_proj[0], "dp"), [])
    expert_of = sum(part_sources("dp"), [])
    expert_of = [lax.axis_index("expert") * lax.axis_size("dp") + place for place in expert_of]
    new_states, *share = mix(
        queries,
        keys_in,
        values_in,
        gate_in,
        beta,
        decay,
        lengths,
        cache,
        norm_gain,
        out_proj,
        tok_local,
    )
    high, low = factors(lax.axis_size("expert"))
    half = high // 2
    middle = half + (high - half) // 2
    groups = [range(half, middle), range(middle, high), range(half)]
    own, rest = scatter_parts(
        [share[step * low : (step + 1) * low] for step in range(high)],
        "expert",
        [*groups[0], *groups[1], *reversed(groups[2])],
    )
    expert_range = jnp.arange(experts_all, dtype=jnp.int32)
    mixing = jnp.sum(
        jnp.where(expert_ids[:, :, None] == expert_range, route_weights[:, :, None], 0.0), axis=1
    )
    coarse = mixing.astype(jnp.bfloat16)
    fine = (mixing - coarse.astype(jnp.float32)).astype(jnp.bfloat16)
    pad = jnp.zeros((tok_local, -2 * experts_all % 128), jnp.bfloat16)
    attn_out, block = close(
        sum_parts([residual, *own]),
        rest,
        post_gain,
        jnp.concatenate([coarse, fine, pad], axis=1),
    )
    gathered = gather_parts(block, "expert", around=True)
    slots = len(gate_up_parts)
    late = max(1, slots - factors(lax.axis_size("dp"))[1] + 1)
    held = [[gate_up_parts[0], down_parts[0]]]
    for part in (slice(1, late), slice(late, slots)):
        arrays = gate_up_parts[part] + down_parts[part]
        held.append(hold(arrays) if arrays else arrays)
    gate_up_parts = sum([list(part[: len(part) // 2]) for part in held], [])
    down_parts = sum([list(part[len(part) // 2 :]) for part in held], [])
    places = jnp.stack(expert_of).astype(jnp.int32)
    results = {}
    for group in groups:
        blocks = [(step, j) for step in group for j in range(low)]
        if blocks:
            outs = experts(
                places,
                [gathered[step][j] for step, j in blocks],
                gate_up_parts,
                down_parts,
                experts_all,
            )
            results.update(zip(blocks, outs))
    own, rest = scatter_parts(
        [[results[step, j] for j in range(low)] for step in range(high)],
        "expert",
        [*groups[0], *groups[1], *reversed(groups[2])],
    )
    moe_out = sum_parts([*own, *rest]).astype(jnp.bfloat16)
    return (moe_out, attn_out, new_states)


def close_kernel(count, base_ref, *refs):
    gain_ref, mixing_ref, attn_ref, block_ref = refs[count:]
    width = attn_ref.shape[1]
    total = sum_parts([base_ref[...]] + [ref[...] for ref in refs[:count]])
    attn_ref[...] = total.astype(jnp.bfloat16)
    stream = attn_ref[...].astype(jnp.float32)
    scale = lax.rsqrt(jnp.mean(stream * stream, axis=-1, keepdims=True) + epsilon)
    block_ref[:, :width] = (stream * scale * gain_ref[...]).astype(jnp.bfloat16)
    block_ref[:, width:] = mixing_ref[...]


def close(base, rest, post_gain, mixing):
    rows, width = base.shape
    vmem = pl.BlockSpec(memory_space=pltpu.VMEM)
    return pl.pallas_call(
        functools.partial(close_kernel, len(rest)),
        in_specs=[vmem] * (len(rest) + 3),
        out_specs=[vmem] * 2,
        out_shape=[
            jax.ShapeDtypeStruct((rows, width), jnp.bfloat16),
            jax.ShapeDtypeStruct((rows, width + mixing.shape[1]), jnp.bfloat16),
        ],
        compiler_params=pltpu.CompilerParams(vmem_limit_bytes=8 << 20),
        name="close",
    )(base, *rest, post_gain[None], mixing)


def hold_kernel(*refs):
    count = (len(refs) - 1) // 2
    loads = [
        pltpu.make_async_copy(refs[n], refs[count + n], refs[-1].at[n]) for n in range(count)
    ]
    for load in loads:
        load.start()
    for load in loads:
        load.wait()


def hold(arrays):
    count = len(arrays)
    return pl.pallas_call(
        hold_kernel,
        in_specs=[pl.BlockSpec(memory_space=pltpu.HBM)] * count,
        out_specs=[pl.BlockSpec(memory_space=pltpu.VMEM)] * count,
        out_shape=[pltpu.VMEM(array.shape, array.dtype) for array in arrays],
        scratch_shapes=[pltpu.SemaphoreType.DMA((count,))],
        compiler_params=pltpu.CompilerParams(vmem_limit_bytes=16 << 20),
        name="hold",
    )(*arrays)


def experts_kernel(blocks, slots, experts_all, places_ref, *refs):
    row_refs = refs[:blocks]
    gate_up_refs = refs[blocks : blocks + slots]
    down_refs = refs[blocks + slots : blocks + 2 * slots]
    out_refs = refs[blocks + 2 * slots : 2 * blocks + 2 * slots]
    hidden_buf = refs[2 * blocks + 2 * slots]
    width, hidden_width = gate_up_refs[0].shape[0], down_refs[0].shape[0]
    rows = jnp.concatenate([ref[:, :width] for ref in row_refs], axis=0)
    mixing = jnp.concatenate([ref[:, width:] for ref in row_refs], axis=0).astype(jnp.float32)
    lane = lax.broadcasted_iota(jnp.int32, mixing.shape, 1)
    for i in range(slots):
        place = places_ref[i]
        named = (lane == place) | (lane == place + experts_all)
        weight = jnp.sum(jnp.where(named, mixing, 0.0), axis=1, keepdims=True)
        both = product(rows, gate_up_refs[i][...])
        gate = both[:, :hidden_width]
        hidden = gate * jax.nn.sigmoid(gate) * both[:, hidden_width:] * weight
        hidden_buf[:, i * hidden_width : (i + 1) * hidden_width] = hidden.astype(jnp.bfloat16)
    size = row_refs[0].shape[0]
    tile = min(512, width)
    for start in range(0, width, tile):
        down = jnp.concatenate([ref[:, start : start + tile] for ref in down_refs], axis=0)
        result = product(hidden_buf[...], down).astype(jnp.bfloat16)
        for n in range(blocks):
            out_refs[n][:, start : start + tile] = result[n * size : (n + 1) * size]


def experts(places, row_blocks, gate_up_parts, down_parts, experts_all):
    blocks, slots = len(row_blocks), len(gate_up_parts)
    size = row_blocks[0].shape[0]
    width, hidden_twice = gate_up_parts[0].shape
    hidden_width = down_parts[0].shape[0]
    vmem = pl.BlockSpec(memory_space=pltpu.VMEM)
    return pl.pallas_call(
        functools.partial(experts_kernel, blocks, slots, experts_all),
        in_specs=[pl.BlockSpec(memory_space=pltpu.SMEM)]
        + [vmem] * (blocks + 2 * slots),
        out_specs=[vmem] * blocks,
        out_shape=[jax.ShapeDtypeStruct((size, width), jnp.bfloat16)] * blocks,
        scratch_shapes=[
            pltpu.VMEM((blocks * size, slots * hidden_width), jnp.bfloat16),
        ],
        cost_estimate=pl.CostEstimate(
            flops=2 * blocks * size * slots * width * (hidden_twice + hidden_width),
            bytes_accessed=4 * blocks * size * width,
            transcendentals=0,
        ),
        compiler_params=pltpu.CompilerParams(
            vmem_limit_bytes=(12 << 20)
            + 2 * slots * width * (hidden_twice + hidden_width)
        ),
        name="experts",
    )(places, *row_blocks, *gate_up_parts, *down_parts)


def solution(mesh):
    return jax.shard_map(
        on_device,
        mesh=mesh,
        in_specs=(
            P(("groups", "dp"), "expert"),
            P(("groups", "dp"), "expert"),
            P(("groups", "dp"), "expert"),
            P(("groups", "dp"), "expert"),
            P(("groups", "dp"), "expert"),
            P(("groups", "dp"), "expert"),
            P(("groups", "dp"), None),
            P(("groups", "dp"), "expert", None, None),
            P(),
            P("expert", None),
            P(("groups", "dp", "expert"), None),
            P(),
            P(("groups", "dp", "expert"), None),
            P(("groups", "dp", "expert"), None),
            P(("expert", "dp"), None, None),
            P(("expert", "dp"), None, None),
        ),
        out_specs=(
            P(("groups", "dp", "expert"), None),
            P(("groups", "dp", "expert"), None),
            P(("groups", "dp"), "expert", None, None),
        ),
        check_vma=False,
    )
```
